512 devices in a mesh: gen: 128 (over z, x, core), split: 4 (over y).
Axes of the slice: x: 4, y: 4, z: 16, core: 2. Of those that a mesh axis runs over, the one named last changes fastest.
Arguments:
- hidden: bfloat16 [32, 4096, 8192], P(None, 'gen', 'split'), may hold values from -12 to 12
- w_proj: bfloat16 [8192, 1024], P('split', 'gen'), may hold values from -0.0625 to 0.0625
- slot_prompt: int32 [4096], P('gen'), may hold values from 0 to 127, as said below
- lengths: int32 [4096], P('gen'), may hold values from 1 to 32
- weights: bfloat16 [4096], P('gen'), may hold values from 0.099609375 to 10
- owner: int32 [128], replicated, may hold values from 0 to 127, each once
Outputs:
- utility: float32 [128, 64], P('gen')
The draws below stay inside these ranges and needn't reach their ends.
Inputs may be any that keep to these rules, and one draw needn't show every extreme that they name: `slot_prompt`: each prompt names 1 to 64 slots and one prompt names exactly 64; each generator device (a run of 32 slots) holds at most 1 slots of one prompt, and some device holds exactly 1. `owner`: each index along gen owns exactly one prompt.
All inputs are finite; a program needn't handle non-finite values.
Results may differ from the reference program's by a relative error of at most 0.0015.
Values may be sent and summed in bfloat16 or wider, within the bound.
No kernel may reach another device: no remote copies, remote signals or barrier semaphores. Data moves between devices by JAX's collectives and lax.ppermute only.
A program may use at most 64 MiB of HBM per device.

```python
import math
import jax
import jax.numpy as jnp
from jax import lax

HID = 8192
EMB = 1024
SEQ = 32
SLOTS = 32
MAXS = 64
NS = 4096
N_GEN = 128
N_SPLIT = 4


def slot_prompts(key):
    heat_key = jax.random.fold_in(key, 11)
    noise_key = jax.random.fold_in(key, 12)
    home_key = jax.random.fold_in(key, 13)
    order_key = jax.random.fold_in(key, 14)
    full_key = jax.random.fold_in(key, 15)
    prompts = N_GEN
    extra = MAXS - 1
    cells = prompts * extra
    heat = jax.random.randint(heat_key, (prompts,), 0, 4)
    full_prompt = jax.random.randint(full_key, (), 0, prompts)
    noise = jax.random.randint(noise_key, (prompts, extra), 0, 2048)
    cell_index = jnp.arange(cells, dtype=jnp.int32).reshape(prompts, extra)
    scores = (heat[:, None] * 2048 + noise) * cells + cell_index
    is_full = jnp.arange(prompts, dtype=jnp.int32) == full_prompt
    scores = jnp.where(is_full[:, None], -1, scores)
    remaining = N_GEN * SLOTS - MAXS - (prompts - 1)
    flat_scores = scores.reshape(cells)
    top_values, top_where = jax.lax.top_k(flat_scores, remaining)
    threshold = top_values[remaining - 1]
    picked = (scores >= threshold).astype(jnp.int32)
    counts = 1 + jnp.sum(picked, axis=1)
    counts = jnp.where(is_full, MAXS, counts)
    ends = jnp.cumsum(counts)
    samples = N_GEN * SLOTS
    home = jax.random.permutation(home_key, N_GEN)
    order_scores = jax.random.randint(order_key, (N_GEN, SLOTS), 0, 2 ** 20) * SLOTS + jnp.arange(SLOTS, dtype=jnp.int32)[None, :]
    arrange = jnp.argsort(order_scores, axis=1)
    residue = jnp.arange(N_GEN, dtype=jnp.int32)[:, None]
    global_index = arrange * N_GEN + residue
    prompt_of = jnp.sum((global_index.reshape(samples)[:, None] >= ends[None, :]).astype(jnp.int32), axis=1)
    target = (home[:, None] * SLOTS + jnp.arange(SLOTS, dtype=jnp.int32)[None, :]).reshape(samples)
    result = jnp.zeros((samples,), jnp.int32).at[target].set(prompt_of)
    return result


def draw_slot_prompt(key, part):
    return slot_prompts(key)


def draw_hidden(key, part):
    prompt_of = slot_prompts(key)
    samples = N_GEN * SLOTS
    direction_count = 12
    direction_pool = jax.random.normal(jax.random.fold_in(key, 21), (N_GEN * direction_count, HID), jnp.float32)
    first_direction = jax.random.randint(jax.random.fold_in(key, 22), (samples,), 0, direction_count)
    direction_span = jax.random.randint(jax.random.fold_in(key, 23), (samples,), 1, direction_count + 1)
    offsets = jax.random.randint(jax.random.fold_in(key, 24), (SEQ, samples), 0, 65536) % direction_span[None, :]
    picked_direction = (first_direction[None, :] + offsets) % direction_count
    chosen = jnp.take(direction_pool, prompt_of[None, :] * direction_count + picked_direction, axis=0)
    noise_level = jnp.exp(jax.random.uniform(jax.random.fold_in(key, 25), (samples,), jnp.float32, math.log(0.3), 0.0))
    amplitude = jax.random.uniform(jax.random.fold_in(key, 26), (SEQ, samples), jnp.float32, 0.7, 1.3)
    noise_part = jax.random.normal(jax.random.fold_in(key, 27), (SEQ, samples, HID), jnp.float32)
    mixture = amplitude[:, :, None] * chosen + noise_level[None, :, None] * noise_part
    return jnp.clip(mixture, -12.0, 12.0).astype(jnp.bfloat16)


def place_ends(values, key, low, largest):
    extent = values.shape
    spot = [jax.random.randint(jax.random.fold_in(key, axis), (), 0, extent[axis]) for axis in range(len(extent))]
    values = values.at[tuple(spot)].set(low)
    longest = extent.index(max(extent))
    spot[longest] = (spot[longest] + 1) % extent[longest]
    return values.at[tuple(spot)].set(largest)


def block_scale(key, extent, pieces, low, high):
    loudness = 1.0
    for dim, parts in pieces:
        steps = jax.random.uniform(jax.random.fold_in(jax.random.fold_in(key, 6), dim), (parts,), jnp.float32, low / len(pieces), high / len(pieces))
        loudness = loudness * jnp.repeat(jnp.exp(steps), extent[dim] // parts).reshape((-1,) + (1,) * (len(extent) - 1 - dim))
    return loudness


def bell_draw(key, shape, width, most, shards=(), kind=jnp.bfloat16):
    array = jax.random.normal(key, shape, jnp.float32) * width
    if len(shards) > 0:
        array = block_scale(key, shape, shards, -0.22, 0.18) * array
    return jnp.clip(array, min=-most, max=most).astype(kind)


def setup_inputs(seed: int = 0) -> dict:
    key_of = jax.random.split(jax.random.key(seed), 7)
    hidden = draw_hidden(jax.random.fold_in(key_of[6], 71), 0)
    w_proj = bell_draw(key_of[1], (HID, EMB), HID ** -0.5, 0.0625, ((0, 4), (1, 128)))
    slot_prompt = draw_slot_prompt(jax.random.fold_in(key_of[6], 71), 0)
    lengths = place_ends(jax.random.randint(key_of[3], (NS,), 1, SEQ + 1), jax.random.fold_in(key_of[3], 1), 1, SEQ).astype(jnp.int32)
    weights = jnp.clip(jnp.exp(math.log(10.0) - 4.609084 * jax.random.uniform(key_of[4], (NS,), jnp.float32) ** block_scale(key_of[4], (NS,), ((0, 128),), -0.2, 0.2)), 0.099609375, 10.0).astype(jnp.bfloat16)
    owner = jax.random.permutation(key_of[5], N_GEN).astype(jnp.int32)
    return {"hidden": hidden, "w_proj": w_proj, "slot_prompt": slot_prompt, "lengths": lengths, "weights": weights, "owner": owner}


def project_group(hidden, w_proj, group_index):
    part_rows = HID // N_SPLIT
    block = lax.dynamic_slice_in_dim(hidden, group_index * SLOTS, SLOTS, 1)
    summed = jnp.zeros((SEQ, SLOTS, EMB), jnp.float32)
    for feature_part in range(N_SPLIT):
        rows_part = block[:, :, feature_part * part_rows:(feature_part + 1) * part_rows].astype(jnp.float32)
        weight_part = w_proj[feature_part * part_rows:(feature_part + 1) * part_rows].astype(jnp.float32)
        partial_term = jnp.einsum('psh,he->pse', rows_part, weight_part)
        rounded = lax.optimization_barrier(partial_term.astype(jnp.bfloat16))
        summed = summed + rounded.astype(jnp.float32)
    scale = lax.rsqrt(lax.optimization_barrier(jnp.mean(summed * summed, axis=-1, keepdims=True)) + 1e-06) / math.sqrt(EMB)
    return (summed * scale).astype(jnp.bfloat16)

def prompt_utility(embedded, slot_prompt, lengths, weights, prompt):
    member = (slot_prompt == prompt).astype(jnp.int32)
    running = jnp.cumsum(member)
    targets = jnp.arange(MAXS, dtype=jnp.int32)
    position = lax.optimization_barrier(jnp.sum((running[None, :] <= targets[:, None]).astype(jnp.int32), axis=1))
    position = jnp.minimum(position, SLOTS * N_GEN - 1).astype(jnp.int32)
    filled = targets < running[-1]
    member_len = jnp.where(filled, jnp.take(lengths, position), 0).astype(jnp.int32)
    member_weight = jnp.where(filled, jnp.take(weights, position).astype(jnp.float32), jnp.float32(0.0))
    chosen = jnp.take(embedded, position, axis=1)
    flat = chosen.reshape(SEQ * MAXS, EMB)
    sim = jnp.dot(flat, flat.T, preferred_element_type=jnp.float32).reshape(SEQ, MAXS, SEQ, MAXS)
    steps_pos = jnp.arange(SEQ, dtype=jnp.int32)
    col_ok = steps_pos[:, None] < member_len[None, :]
    sim = jnp.where(col_ok[None, None, :, :], sim, jnp.float32(-2.0))
    best = lax.optimization_barrier(jnp.max(sim, axis=2))
    row_ok = steps_pos[:, None] < member_len[None, :]
    summed = lax.optimization_barrier(jnp.sum(jnp.where(row_ok[:, :, None], best, jnp.float32(0.0)), axis=0))
    recall = summed / jnp.maximum(member_len, 1).astype(jnp.float32)[:, None]
    score = 0.5 * (recall + recall.T)
    util = lax.optimization_barrier(jnp.sum(score * member_weight[None, :], axis=1)) / jnp.sum(member_weight)
    return jnp.where(filled, util, jnp.float32(0.0))

def reference(hidden, w_proj, slot_prompt, lengths, weights, owner):
    groups = lax.map(lambda group_index: project_group(hidden, w_proj, group_index), jnp.arange(N_GEN, dtype=jnp.int32))
    embedded = jnp.transpose(groups, (1, 0, 2, 3)).reshape(SEQ, N_GEN * SLOTS, EMB)
    per_prompt = lax.map(lambda prompt: prompt_utility(embedded, slot_prompt, lengths, weights, prompt), jnp.arange(N_GEN, dtype=jnp.int32))
    table = jnp.zeros((N_GEN, MAXS), jnp.float32)
    return table.at[owner].set(per_prompt)
```

```python
import math

import jax
import jax.numpy as jnp
from jax import lax
from jax.experimental import pallas as pl
from jax.experimental.pallas import tpu as pltpu
from jax.sharding import Mesh
from jax.sharding import PartitionSpec as P

MAXS = 64
SEQ = 32
EMB = 1024
NZ, NX, NC, NY = 16, 4, 2, 4
GEN = NZ * NX * NC
SLOTS = 32
HB = 2048
BF = jnp.bfloat16
F32 = jnp.float32
I32 = jnp.int32


def shift(v, axis, n, k):
    return lax.ppermute(v, axis, [(i, (i + k) % n) for i in range(n)])


def swap(v, axis, n, d):
    return lax.ppermute(v, axis, [(i, i ^ d) for i in range(n)])


def two_way_ring(v, axis, n):
    half = v.shape[0] // 2
    before = shift(v, axis, n, 1)
    after = shift(v, axis, n, n - 1)
    low = shift(before[:half], axis, n, 1)
    high = shift(after[half:], axis, n, n - 1)
    return [v, before, after, jnp.concatenate([low, high])]


RING = (0, NY - 1, 1, 2)


def utility_kernel(x_ref, col_ref, row_ref, len_ref, w_ref, out_ref, xn_ref, acc_ref):
    i = pl.program_id(0)
    blk = 256

    @pl.when(i == 0)
    def _():
        acc_ref[...] = jnp.zeros_like(acc_ref)

        def norm(b, carry):
            v = x_ref[pl.ds(b * blk, blk), :].astype(F32)
            s = lax.rsqrt(jnp.sum(v * v, axis=1, keepdims=True) * (1.0 / EMB) + 1e-6) * (1.0 / math.sqrt(EMB))
            xn_ref[pl.ds(b * blk, blk), :] = (v * s).astype(BF)
            return carry

        lax.fori_loop(0, SEQ * MAXS // blk, norm, 0)

    rows = xn_ref[pl.ds(i * blk, blk), :]
    best = jnp.full((blk, 128), -2.0, F32)
    for q in range(4):
        cols = xn_ref[q * 512 : (q + 1) * 512, :]
        s = lax.dot_general(rows, cols, (((1,), (1,)), ((), ())), preferred_element_type=F32)
        for k in range(4):
            ok = col_ref[q * 4 + k : q * 4 + k + 1, :] > 0
            best = jnp.maximum(best, jnp.where(ok, s[:, k * 128 : (k + 1) * 128], -2.0))
    best = jnp.maximum(best[:, :MAXS], best[:, MAXS:])
    best = jnp.where(row_ref[...] > 0, best, 0.0)
    acc_ref[...] += jnp.sum(best.reshape(blk // MAXS, MAXS, MAXS), axis=0)

    @pl.when(i == pl.num_programs(0) - 1)
    def _():
        recall = acc_ref[...] / jnp.maximum(len_ref[...], 1.0)
        score = 0.5 * (recall + recall.T)
        util = jnp.sum(score * w_ref[...], axis=0, keepdims=True) / jnp.sum(w_ref[...])
        out_ref[...] = util


def utility(x, ok, member_len, member_weight):
    okf = ok.astype(F32)
    n = SEQ * MAXS
    blk = 256
    return pl.pallas_call(
        utility_kernel,
        grid=(n // blk,),
        in_specs=[
            pl.BlockSpec((n, EMB), lambda i: (0, 0)),
            pl.BlockSpec((n // 128, 128), lambda i: (0, 0)),
            pl.BlockSpec((blk, 1), lambda i: (i, 0)),
            pl.BlockSpec((MAXS, 1), lambda i: (0, 0)),
            pl.BlockSpec((MAXS, 1), lambda i: (0, 0)),
        ],
        out_specs=pl.BlockSpec((1, MAXS), lambda i: (0, 0)),
        out_shape=jax.ShapeDtypeStruct((1, MAXS), F32),
        scratch_shapes=[pltpu.VMEM((n, EMB), BF), pltpu.VMEM((MAXS, MAXS), F32)],
        compiler_params=pltpu.CompilerParams(vmem_limit_bytes=48 << 20),
    )(x, okf.reshape(n // 128, 128), okf.reshape(n, 1), member_len.astype(F32)[:, None], member_weight[:, None])


def body(hidden, w_proj, slot_prompt, lengths, weights, owner):
    z, x, c, y = (lax.axis_index(a) for a in ("z", "x", "c", "y"))
    me = (z * NX + x) * NC + c

    meta = jnp.concatenate([slot_prompt.astype(BF), lengths.astype(BF), weights, jnp.zeros((32,), BF)])
    part = jnp.concatenate([w_proj.T, jnp.broadcast_to(meta[None, :], (8, 128))], axis=1)
    for d in (8, 4, 2, 1):
        other = swap(part, "z", NZ, d)
        bit = (z // d) % 2 == 1
        part = jnp.concatenate([jnp.where(bit, other, part), jnp.where(bit, part, other)])
    rows = hidden.reshape(SEQ * SLOTS, HB)
    projected = jnp.zeros((NX, SEQ * SLOTS, NC * 128), BF)
    metas = jnp.zeros((NX, NC, NZ, 128), BF)
    for k, chunk in zip(RING, two_way_ring(part, "x", NX)):
        other = swap(chunk, "c", NC, 1)
        both = jnp.concatenate([jnp.where(c == 1, other, chunk), jnp.where(c == 1, chunk, other)])
        term = lax.dot_general(rows, both[:, :HB], (((1,), (1,)), ((), ())), preferred_element_type=F32)
        at = (x + k) % NX
        projected = lax.dynamic_update_slice(projected, term.astype(BF)[None], (at, 0, 0))
        metas = lax.dynamic_update_slice(metas, both[:, HB:].reshape(1, NC, NZ, 8, 128)[:, :, :, 0], (at, 0, 0, 0))
    metas = metas.reshape(NX, NC, 2, 2, 2, 2, 128).transpose(5, 4, 3, 2, 0, 1, 6).reshape(GEN, 128)
    all_prompt = metas[:, :32].astype(I32)
    all_len = metas[:, 32:64].astype(I32)
    all_weight = metas[:, 64:96].astype(F32)

    by_pos = projected.reshape(NX, NY, SEQ // NY * SLOTS, NC * 128)
    total = lax.dynamic_index_in_dim(by_pos, y, 1, keepdims=False).astype(F32)
    for k in (1, 3, 2):
        piece = lax.dynamic_index_in_dim(by_pos, (y + k) % NY, 1, keepdims=False)
        total = total + shift(piece, "y", NY, k).astype(F32)
    emb = total.astype(BF).transpose(1, 0, 2).reshape(SEQ // NY * SLOTS, EMB)

    gens = jnp.arange(GEN, dtype=I32)
    dest = jnp.sum(jnp.where(slot_prompt[:, None] == gens[None, :], owner[None, :], 0), axis=1)
    n_pos = SEQ // NY
    out_row = jnp.arange(GEN * n_pos, dtype=I32)
    in_row_dest = jnp.broadcast_to(dest[None, :], (n_pos, SLOTS)).reshape(-1)
    in_row_pos = jnp.broadcast_to(jnp.arange(n_pos, dtype=I32)[:, None], (n_pos, SLOTS)).reshape(-1)
    pick = (out_row[:, None] == (in_row_dest * n_pos + in_row_pos)[None, :]).astype(BF)
    send = jnp.dot(pick, emb, preferred_element_type=F32).astype(BF).reshape(GEN, n_pos, EMB)
    arrived = lax.all_to_all(send, ("z", "x", "c"), split_axis=0, concat_axis=0, tiled=True)

    prompt = jnp.sum(jnp.where(owner == me, gens, 0))
    hit = all_prompt == prompt
    present = jnp.any(hit, axis=1)
    len_of = jnp.sum(jnp.where(hit, all_len, 0), axis=1)
    weight_of = jnp.sum(jnp.where(hit, all_weight, 0.0), axis=1)
    rank = jnp.sum((present[None, :] & (gens[None, :] < gens[:, None])).astype(I32), axis=1)
    rank = jnp.where(present, rank, -1)
    is_member = jnp.arange(MAXS, dtype=I32)[:, None] == rank[None, :]
    member_len = jnp.sum(jnp.where(is_member, len_of[None, :], 0), axis=1)
    member_weight = jnp.sum(jnp.where(is_member, weight_of[None, :], 0.0), axis=1)
    src_pos = jnp.broadcast_to(jnp.arange(n_pos, dtype=I32)[None, :], (GEN, n_pos)).reshape(-1)
    src_rank = jnp.broadcast_to(rank[:, None], (GEN, n_pos)).reshape(-1)
    src_at = jnp.where(src_rank >= 0, src_pos * MAXS + src_rank, -1)
    pick = (jnp.arange(n_pos * MAXS, dtype=I32)[:, None] == src_at[None, :]).astype(BF)
    mine = jnp.dot(pick, arrived.reshape(GEN * n_pos, EMB), preferred_element_type=F32).astype(BF)

    ring = two_way_ring(mine, "y", NY)
    tokens = jnp.concatenate(ring)
    pos = jnp.concatenate([((y + k) % NY) * n_pos + jnp.arange(n_pos, dtype=I32) for k in RING])
    ok = pos[:, None] < member_len[None, :]
    util = utility(tokens, ok, member_len, member_weight)
    return jnp.where(jnp.arange(MAXS, dtype=I32)[None, :] < jnp.sum(present.astype(I32)), util, 0.0)


def solution(mesh):
    fine = Mesh(mesh.devices.reshape(NZ, NX, NC, NY), ("z", "x", "c", "y"))
    g = ("z", "x", "c")
    placed = (P(None, g, "y"), P("y", g), P(g), P(g), P(g), P())
    return jax.shard_map(body, mesh=fine, in_specs=placed, out_specs=P(g, None), check_vma=False)
```

```python
import functools
import math

import jax
import jax.numpy as jnp
from jax import lax
from jax.experimental import pallas as pl
from jax.experimental.pallas import tpu as pltpu
from jax.sharding import Mesh
from jax.sharding import PartitionSpec as P

MAXS = 64
SEQ = 32
EMB = 1024
NZ, NX, NC, NY = 16, 4, 2, 4
GEN = NZ * NX * NC
SLOTS = 32
HB = 2048
BF = jnp.bfloat16
F32 = jnp.float32
I32 = jnp.int32
POS = SEQ // NY
CT = 192
ROOM = ((160, 320), (208, 352))
KT, KO = ROOM[-1]
FAR = 1024


def shift(v, axis, n, k):
    return lax.ppermute(v, axis, [(i, (i + k) % n) for i in range(n)])


def swap(v, axis, n, d):
    return lax.ppermute(v, axis, [(i, i ^ d) for i in range(n)])


def two_way_ring(v, axis, n):
    half = v.shape[0] // 2
    before = shift(v, axis, n, 1)
    after = shift(v, axis, n, n - 1)
    low = shift(before[:half], axis, n, 1)
    high = shift(after[half:], axis, n, n - 1)
    return [v, before, after, jnp.concatenate([low, high])]


RING = (0, NY - 1, 1, 2)


def similarity(i, xn_ref, col_ref, row_ref, len_ref, w_ref, out_ref, acc_ref):
    blk = 256

    @pl.when(i == 0)
    def _():
        acc_ref[...] = jnp.zeros_like(acc_ref)

    rows = xn_ref[pl.ds(pl.multiple_of(i * blk, blk), blk), :]
    best = jnp.full((blk, 128), -2.0, F32)
    for q in range(4):
        cols = xn_ref[q * 512 : (q + 1) * 512, :]
        s = lax.dot_general(rows, cols, (((1,), (1,)), ((), ())), preferred_element_type=F32)
        for k in range(4):
            ok = col_ref[q * 4 + k : q * 4 + k + 1, :] > 0
            best = jnp.maximum(best, jnp.where(ok, s[:, k * 128 : (k + 1) * 128], -2.0))
    best = jnp.maximum(best[:, :MAXS], best[:, MAXS:])
    best = jnp.where(row_ref[...] > 0, best, 0.0)
    acc_ref[...] += jnp.sum(best.reshape(blk // MAXS, MAXS, MAXS), axis=0)

    @pl.when(i == pl.num_programs(0) - 1)
    def _():
        recall = acc_ref[...] / jnp.maximum(len_ref[...], 1.0)
        score = 0.5 * (recall + recall.T)
        out_ref[...] = jnp.sum(score * w_ref[...], axis=0, keepdims=True) / jnp.sum(w_ref[...])


def unit(v):
    s = lax.rsqrt(jnp.sum(v * v, axis=1, keepdims=True) * (1.0 / EMB) + 1e-6) * (1.0 / math.sqrt(EMB))
    return (v * s).astype(BF)


def utility_kernel(x_ref, col_ref, row_ref, len_ref, w_ref, out_ref, xn_ref, acc_ref):
    i = pl.program_id(0)

    @pl.when(i == 0)
    def _():
        def norm(b, carry):
            at = pl.ds(pl.multiple_of(b * 256, 256), 256)
            xn_ref[at, :] = unit(x_ref[at, :].astype(F32))
            return carry

        lax.fori_loop(0, SEQ * MAXS // 256, norm, 0)

    similarity(i, xn_ref, col_ref, row_ref, len_ref, w_ref, out_ref, acc_ref)


def packed_utility_kernel(x_ref, at_ref, col_ref, row_ref, len_ref, w_ref, out_ref, xn_ref, acc_ref):
    i = pl.program_id(0)

    @pl.when(i == 0)
    def _():
        for q in range(NY):
            vals = jnp.concatenate([x_ref[g * NY + q] for g in range(NX * NC)], axis=1)
            slot = lax.broadcasted_iota(I32, (POS * MAXS, at_ref.shape[1]), 0)
            pick = jnp.where(slot == at_ref[q : q + 1, :], 1.0, 0.0).astype(BF)
            v = jnp.dot(pick, vals, preferred_element_type=F32)
            xn_ref[q * POS * MAXS : (q + 1) * POS * MAXS, :] = unit(v)

    similarity(i, xn_ref, col_ref, row_ref, len_ref, w_ref, out_ref, acc_ref)


def utility(x, ok, member_len, member_weight, at=None):
    okf = ok.astype(F32)
    n = SEQ * MAXS
    blk = 256
    whole = lambda a: pl.BlockSpec(a.shape, lambda i, d=a.ndim: (0,) * d)
    ins = [x] + ([] if at is None else [at]) + [okf.reshape(n // 128, 128)]
    small = [member_len.astype(F32)[:, None], member_weight[:, None]]
    return pl.pallas_call(
        utility_kernel if at is None else packed_utility_kernel,
        grid=(n // blk,),
        in_specs=[whole(a) for a in ins] + [pl.BlockSpec((blk, 1), lambda i: (i, 0))] + [whole(a) for a in small],
        out_specs=pl.BlockSpec((1, MAXS), lambda i: (0, 0)),
        out_shape=jax.ShapeDtypeStruct((1, MAXS), F32),
        scratch_shapes=[pltpu.VMEM((n, EMB), BF), pltpu.VMEM((MAXS, MAXS), F32)],
        compiler_params=pltpu.CompilerParams(vmem_limit_bytes=48 << 20),
    )(*ins, okf.reshape(n, 1), *small)


def project_kernel(where_ref, rows_ref, mate_ref, w_ref, *refs):
    out_ref, meta_ref = refs[-2:]
    c = where_ref[1]
    for r_ref, e in ((rows_ref, c), (mate_ref, 1 - c)):
        term = lax.dot_general(r_ref[...], w_ref[:, :HB], (((1,), (1,)), ((), ())), preferred_element_type=F32)
        for q in range(NY):
            out_ref[0, q, e] = term[q * CT : (q + 1) * CT, :].astype(BF)
    meta_ref[0] = w_ref[:, HB:]


def project(where, rows, mate, w, into):
    blocks = (1, NY, NC, CT, 128), (1, 128, 128)
    whole = lambda a: pl.BlockSpec(a.shape, lambda i, at: (0, 0))
    old = [] if into is None else list(into)
    return pl.pallas_call(
        project_kernel,
        grid_spec=pltpu.PrefetchScalarGridSpec(
            num_scalar_prefetch=1,
            grid=(1,),
            in_specs=[whole(rows), whole(mate), whole(w)] + [pl.BlockSpec(memory_space=pl.ANY) for _ in old],
            out_specs=[pl.BlockSpec(b, lambda i, at, d=len(b): (at[0],) + (0,) * (d - 1)) for b in blocks],
        ),
        out_shape=[jax.ShapeDtypeStruct((NX,) + b[1:], BF) for b in blocks],
        input_output_aliases={4: 0, 5: 1} if old else {},
        compiler_params=pltpu.CompilerParams(vmem_limit_bytes=32 << 20),
    )(where, rows, mate, w, *old)


def sum_pack_kernel(x_ref, at_ref, out_ref, v_ref):
    i = pl.program_id(0)
    some, room = out_ref.shape[:2]

    @pl.when(i == 0)
    def _():
        for g in range(NX):
            for e in range(NC):
                v = x_ref[g * NY, e].astype(F32)
                for q in range(1, NY):
                    v = v + x_ref[g * NY + q, e].astype(F32)
                n = g * NC + e
                v_ref[n * CT : (n + 1) * CT, :] = v.astype(BF)

    for b in range(some):
        slot = lax.broadcasted_iota(I32, (room, NX * NC * CT), 0) + (i * some + b) * FAR
        pick = jnp.where(slot == at_ref[...], 1.0, 0.0).astype(BF)
        out_ref[b] = jnp.dot(pick, v_ref[...], preferred_element_type=F32).astype(BF)


def sum_pack(x, at, room):
    n = NX * NC * CT
    some = 4
    return pl.pallas_call(
        sum_pack_kernel,
        grid=(NZ // some,),
        in_specs=[pl.BlockSpec(x.shape, lambda i: (0, 0, 0, 0)), pl.BlockSpec((1, n), lambda i: (0, 0))],
        out_specs=pl.BlockSpec((some, room, 128), lambda i: (i, 0, 0)),
        out_shape=jax.ShapeDtypeStruct((NZ, room, 128), BF),
        scratch_shapes=[pltpu.VMEM((n, 128), BF)],
        compiler_params=pltpu.CompilerParams(vmem_limit_bytes=40 << 20),
    )(x, at.reshape(1, n))


def repack_kernel(x_ref, at_ref, out_ref):
    i = pl.program_id(0)
    some, _, room = out_ref.shape[:3]
    for b in range(some):
        slot = lax.broadcasted_iota(I32, (room, x_ref.shape[0]), 0) + (i * some + b) * FAR
        pick = jnp.where(slot == at_ref[...], 1.0, 0.0).astype(BF)
        v = jnp.dot(pick, x_ref[...], preferred_element_type=F32).astype(BF)
        for q in range(NY):
            out_ref[b, q] = v


def repack(x, at, room):
    n = x.shape[0] * x.shape[1]
    some = 2
    return pl.pallas_call(
        repack_kernel,
        grid=(NX * NC // some,),
        in_specs=[pl.BlockSpec((n, 128), lambda i: (0, 0)), pl.BlockSpec((1, n), lambda i: (0, 0))],
        out_specs=pl.BlockSpec((some, NY, room, 128), lambda i: (i, 0, 0, 0)),
        out_shape=jax.ShapeDtypeStruct((NX * NC, NY, room, 128), BF),
        compiler_params=pltpu.CompilerParams(vmem_limit_bytes=40 << 20),
    )(x.reshape(n, 128), at.reshape(1, n))


def before(n):
    i = jnp.arange(n, dtype=I32)
    return i[:, None] < i[None, :]


def prefix(v):
    return jnp.dot(v.astype(BF), before(v.shape[-1]).astype(BF), preferred_element_type=F32).astype(I32)


def uncompacted(x, y, rows, chunks, dest, all_dest, member):
    rank, member_len, member_weight = member
    projected = jnp.zeros((NX, SEQ * SLOTS, NC * 128), BF)
    c = lax.axis_index("c")
    for k, chunk in zip(RING, chunks):
        other = swap(chunk, "c", NC, 1)
        both = jnp.concatenate([jnp.where(c == 1, other, chunk), jnp.where(c == 1, chunk, other)])
        term = lax.dot_general(rows, both[:, :HB], (((1,), (1,)), ((), ())), preferred_element_type=F32)
        projected = lax.dynamic_update_slice(projected, term.astype(BF)[None], ((x + k) % NX, 0, 0))

    by_pos = projected.reshape(NX, NY, POS * SLOTS, NC * 128)
    total = lax.dynamic_index_in_dim(by_pos, y, 1, keepdims=False).astype(F32)
    for k in (1, 3, 2):
        piece = lax.dynamic_index_in_dim(by_pos, (y + k) % NY, 1, keepdims=False)
        total = total + shift(piece, "y", NY, k).astype(F32)
    emb = total.astype(BF).transpose(1, 0, 2).reshape(POS * SLOTS, EMB)

    out_row = jnp.arange(GEN * POS, dtype=I32)
    in_row = jnp.arange(POS, dtype=I32)[:, None] + dest[None, :] * POS
    pick = (out_row[:, None] == in_row.reshape(1, -1)).astype(BF)
    send = jnp.dot(pick, emb, preferred_element_type=F32).astype(BF).reshape(GEN, POS, EMB)
    arrived = lax.all_to_all(send, ("z", "x", "c"), split_axis=0, concat_axis=0, tiled=True)
    src_at = jnp.where(rank[:, None] >= 0, jnp.arange(POS, dtype=I32)[None, :] * MAXS + rank[:, None], -1)
    pick = (jnp.arange(POS * MAXS, dtype=I32)[:, None] == src_at.reshape(1, -1)).astype(BF)
    mine = jnp.dot(pick, arrived.reshape(GEN * POS, EMB), preferred_element_type=F32).astype(BF)

    tokens = jnp.concatenate(two_way_ring(mine, "y", NY))
    pos = jnp.concatenate([((y + k) % NY) * POS + jnp.arange(POS, dtype=I32) for k in RING])
    return utility(tokens, pos[:, None] < member_len[None, :], member_len, member_weight)


def body(hidden, w_proj, slot_prompt, lengths, weights, owner):
    z, x, c, y = (lax.axis_index(a) for a in ("z", "x", "c", "y"))
    me = (z * NX + x) * NC + c
    gens = jnp.arange(GEN, dtype=I32)
    dest = jnp.sum(jnp.where(slot_prompt[:, None] == gens[None, :], owner[None, :], 0), axis=1)

    rows = hidden.reshape(SEQ * SLOTS, HB)
    start = jnp.sum(jnp.where(before(SLOTS), lengths[:, None], 0), axis=0)
    t = jnp.arange(SEQ, dtype=I32)[:, None]
    at = t + start[None, :]
    at = jnp.where(t < lengths[None, :], (at % NY) * CT + at // NY, -1)
    at = jnp.where(start[None, :] + t < NY * CT, at, -1)
    pick = (jnp.arange(NY * CT, dtype=I32)[:, None] == at.reshape(1, -1)).astype(BF)
    packed = jnp.dot(pick, rows, preferred_element_type=F32).astype(BF)
    mate = swap(packed, "c", NC, 1)

    meta = jnp.concatenate([dest.astype(BF), lengths.astype(BF), weights, jnp.zeros((32,), BF)])[None, :]
    twin = swap(meta, "c", NC, 1)
    meta = jnp.concatenate([jnp.where(c == 1, twin, meta), jnp.where(c == 1, meta, twin), jnp.zeros((6, 128), BF)])
    part = jnp.concatenate([w_proj.T, meta], axis=1)
    for d in (8, 4, 2, 1):
        other = swap(part, "z", NZ, d)
        bit = (z // d) % 2 == 1
        part = jnp.concatenate([jnp.where(bit, other, part), jnp.where(bit, part, other)])
    made = None
    chunks = two_way_ring(part, "x", NX)
    for k, chunk in zip(RING, chunks):
        made = project(jnp.stack([(x + k) % NX, c]).astype(I32), packed, mate, chunk, made)
    send, metas = made
    summands = lax.all_to_all(
        send.reshape(NX * NY, NC, CT, 128), ("x", "y"), split_axis=0, concat_axis=0, tiled=True
    )

    metas = metas.reshape(NX, 2, 2, 2, 2, 8, 128)[:, :, :, :, :, :NC]
    metas = metas.transpose(4, 3, 2, 1, 0, 5, 6).reshape(GEN, 128)
    all_dest = metas[:, :32].astype(I32)
    all_len = metas[:, 32:64].astype(I32)
    all_weight = metas[:, 64:96].astype(F32)
    off = prefix(all_len)

    hit = all_dest == me
    present = jnp.any(hit, axis=1)
    rank = jnp.sum((present[:, None] & before(GEN)).astype(I32), axis=0)
    rank = jnp.where(present, rank, -1)
    is_member = jnp.arange(MAXS, dtype=I32)[:, None] == rank[None, :]
    of_member = lambda v, zero: jnp.sum(
        jnp.where(is_member, jnp.sum(jnp.where(hit, v, zero), axis=1)[None, :], zero), axis=1
    )
    member_len, member_off, member_weight = of_member(all_len, 0), of_member(off, 0), of_member(all_weight, 0.0)

    ys = jnp.arange(NY, dtype=I32)[:, None, None]
    on_row = (((off + all_len)[None] + 3 - ys) >> 2) - ((off[None] + 3 - ys) >> 2)
    on_row = on_row.reshape(NY, NZ, NX * NC * SLOTS)
    goes = (all_dest.reshape(NZ, -1)[:, :, None] == gens[None, None, :]).astype(BF)
    load = jnp.einsum("yza,zad->yzd", on_row.astype(BF), goes, preferred_element_type=F32)
    most_along = jnp.max(jnp.sum(load.reshape(NY, NZ, NZ, NX * NC), axis=3))
    most_owned = jnp.max(jnp.sum(load, axis=1))
    fits = jnp.max(off[:, -1] + all_len[:, -1]) <= NY * CT
    choice = sum(jnp.where(fits & (most_along <= a) & (most_owned <= b), 0, 1) for a, b in ROOM)

    lo = (off + 3 - y) >> 2
    hi = (off + all_len + 3 - y) >> 2
    flat = lambda v: v.reshape(NZ, NX * NC * SLOTS)
    n, dz, do = flat(hi - lo), flat(all_dest) // (NX * NC), flat(all_dest) % (NX * NC)
    here = lambda v: lax.dynamic_index_in_dim(v, z, 0, keepdims=False)
    n0, d0 = here(n), here(dz)
    base = jnp.sum(jnp.where(before(n0.shape[0]) & (d0[:, None] == d0[None, :]), n0[:, None], 0), axis=0)
    add = (d0 * FAR + base - here(flat(lo))).reshape(NX * NC, SLOTS, 1)
    j = jnp.arange(CT, dtype=I32)[None, None, :]
    lo0, hi0 = (here(v.reshape(NZ, NX * NC, SLOTS))[:, :, None] for v in (lo, hi))
    at1 = jnp.sum(jnp.where((j >= lo0) & (j < hi0), add + j + 1, 0), axis=1) - 1
    n1 = jnp.where(dz == z, n, 0)
    base1 = prefix(n1)
    o = jnp.arange(NX * NC, dtype=I32)[None, :, None]
    by_owner = jnp.where(do[:, None, :] == o, n1[:, None, :], 0)
    earlier = jnp.sum(jnp.where(before(NZ)[:, :, None], jnp.sum(by_owner, axis=2)[:, None, :], 0), axis=0)
    base2 = prefix(by_owner) + earlier[:, :, None]
    base2 = jnp.sum(jnp.where(do[:, None, :] == o, base2, 0), axis=1)
    add = (do * FAR + base2 - base1)[:, :, None]
    k = jnp.arange(KT, dtype=I32)[None, None, :]
    inside = (k >= base1[:, :, None]) & (k < (base1 + n1)[:, :, None])
    at2 = jnp.sum(jnp.where(inside, add + k + 1, 0), axis=1) - 1
    yy = ys[:, :, 0]
    nm = ((member_off + member_len)[None] + 3 - yy) // 4 - (member_off[None] + 3 - yy) // 4
    basem = prefix(nm)[:, :, None]
    k = jnp.arange(KO, dtype=I32)[None, None, :]
    m = jnp.arange(MAXS, dtype=I32)[None, :, None]
    inside = (k >= basem) & (k < basem + nm[:, :, None])
    at3 = jnp.sum(jnp.where(inside, (k - basem) * MAXS + m + 1, 0), axis=1) - 1
    ok = (jnp.arange(POS, dtype=I32)[None, :, None] < nm[:, None, :]).reshape(SEQ, MAXS)

    def compacted(kt, ko):
        along = lax.all_to_all(sum_pack(summands, at1, kt), "z", split_axis=0, concat_axis=0, tiled=True)
        parts = repack(along, at2[:, :kt], ko).reshape(NX * NC * NY, ko, 128)
        tokens = lax.all_to_all(parts, ("x", "c", "y"), split_axis=0, concat_axis=0, tiled=True)
        return utility(tokens, ok, member_len, member_weight, at3[:, :ko])

    def as_they_are():
        return uncompacted(x, y, rows, chunks, dest, all_dest, (rank, member_len, member_weight))

    util = lax.switch(choice, [functools.partial(compacted, *r) for r in ROOM] + [as_they_are])
    return jnp.where(jnp.arange(MAXS, dtype=I32)[None, :] < jnp.sum(present.astype(I32)), util, 0.0)


def solution(mesh):
    fine = Mesh(mesh.devices.reshape(NZ, NX, NC, NY), ("z", "x", "c", "y"))
    g = ("z", "x", "c")
    placed = (P(None, g, "y"), P("y", g), P(g), P(g), P(g), P())
    return jax.shard_map(body, mesh=fine, in_specs=placed, out_specs=P(g, None), check_vma=False)
```

```python
import functools
import math

import jax
import jax.numpy as jnp
from jax import lax
from jax.experimental import pallas as pl
from jax.experimental.pallas import tpu as pltpu
from jax.sharding import Mesh
from jax.sharding import PartitionSpec as P

MAXS = 64
SEQ = 32
EMB = 1024
NZ, NX, NC, NY = 16, 4, 2, 4
GEN = NZ * NX * NC
SLOTS = 32
HB = 2048
BF = jnp.bfloat16
F32 = jnp.float32
I32 = jnp.int32
POS = SEQ // NY
CT = 192
ROOM = ((160, 320), (208, 352))
KT, KO = ROOM[-1]
FAR = 1024


def shift(v, axis, n, k):
    return lax.ppermute(v, axis, [(i, (i + k) % n) for i in range(n)])


def swap(v, axis, n, d):
    return lax.ppermute(v, axis, [(i, i ^ d) for i in range(n)])


def two_way_ring(v, axis, n):
    half = v.shape[0] // 2
    before = shift(v, axis, n, 1)
    after = shift(v, axis, n, n - 1)
    low = shift(before[:half], axis, n, 1)
    high = shift(after[half:], axis, n, n - 1)
    return [v, before, after, low, high]


RING = (0, NY - 1, 1, 2)


def best_match(rows, cols_ref, col_ref):
    best = jnp.full((rows.shape[0], 128), -2.0, F32)
    for q in range(4):
        cols = cols_ref[q * 512 : (q + 1) * 512, :]
        s = lax.dot_general(rows, cols, (((1,), (1,)), ((), ())), preferred_element_type=F32)
        for k in range(4):
            ok = col_ref[q * 4 + k : q * 4 + k + 1, :] > 0
            best = jnp.maximum(best, jnp.where(ok, s[:, k * 128 : (k + 1) * 128], -2.0))
    return jnp.maximum(best[:, :MAXS], best[:, MAXS:])


def finish(acc_ref, live_ref, len_ref, w_ref, out_ref):
    recall = acc_ref[...] / jnp.maximum(len_ref[...], 1.0)
    score = 0.5 * (recall + recall.T)
    util = jnp.sum(score * w_ref[...], axis=0, keepdims=True) / jnp.sum(w_ref[...])
    out_ref[...] = jnp.where(live_ref[...] > 0, util, 0.0)


def unit(v):
    s = lax.rsqrt(jnp.sum(v * v, axis=1, keepdims=True) * (1.0 / EMB) + 1e-6) * (1.0 / math.sqrt(EMB))
    return (v * s).astype(BF)


def utility_kernel(x_ref, row_ref, col_ref, live_ref, len_ref, w_ref, out_ref, xn_ref, acc_ref):
    i = pl.program_id(0)
    blk = row_ref.shape[0]

    @pl.when(i == 0)
    def _():
        acc_ref[...] = jnp.zeros_like(acc_ref)

        def norm(b, carry):
            at = pl.ds(pl.multiple_of(b * blk, blk), blk)
            xn_ref[at, :] = unit(x_ref[at, :].astype(F32))
            return carry

        lax.fori_loop(0, SEQ * MAXS // blk, norm, 0)

    best = best_match(xn_ref[pl.ds(pl.multiple_of(i * blk, blk), blk), :], xn_ref, col_ref)
    best = jnp.where(row_ref[...] > 0, best, 0.0)
    acc_ref[...] += jnp.sum(best.reshape(blk // MAXS, MAXS, MAXS), axis=0)

    @pl.when(i == pl.num_programs(0) - 1)
    def _():
        finish(acc_ref, live_ref, len_ref, w_ref, out_ref)


def packed_utility_kernel(x_ref, at_ref, col_ref, live_ref, len_ref, w_ref, out_ref, rows_ref, cols_ref, acc_ref):
    i = pl.program_id(0)
    room = at_ref.shape[2]

    @pl.when(i == 0)
    def _():
        acc_ref[...] = jnp.zeros_like(acc_ref)
        for q in range(NY):
            v = jnp.concatenate([x_ref[g * NY + q] for g in range(NX * NC)], axis=1)
            v = unit(v.astype(F32))
            rows_ref[q] = v
            slot = lax.broadcasted_iota(I32, (POS * MAXS, room), 0)
            pick = jnp.where(slot == at_ref[q], 1.0, 0.0).astype(BF)
            v = jnp.dot(pick, v, preferred_element_type=F32)
            cols_ref[q * POS * MAXS : (q + 1) * POS * MAXS, :] = v.astype(BF)

    best = best_match(rows_ref[i], cols_ref, col_ref)
    at = at_ref[i]
    mine = (lax.broadcasted_iota(I32, (MAXS, room), 0) == at % MAXS) & (at >= 0)
    acc_ref[...] += jnp.dot(
        jnp.where(mine, 1.0, 0.0), best, precision=lax.Precision.HIGHEST, preferred_element_type=F32
    )

    @pl.when(i == pl.num_programs(0) - 1)
    def _():
        finish(acc_ref, live_ref, len_ref, w_ref, out_ref)


def utility(x, ok, member_len, member_weight, at=None):
    n = SEQ * MAXS
    whole = lambda a: pl.BlockSpec(a.shape, lambda i, d=a.ndim: (0,) * d)
    live = (member_len > 0).astype(F32)[None, :]
    small = [ok.astype(F32).reshape(n // 128, 128), live, member_len.astype(F32)[:, None], member_weight[:, None]]
    scratch = [pltpu.VMEM((n, EMB), BF), pltpu.VMEM((MAXS, MAXS), F32)]
    if at is None:
        kernel, steps = utility_kernel, 8
        side, spec = ok.astype(F32).reshape(n, 1), pl.BlockSpec((n // steps, 1), lambda i: (i, 0))
    else:
        kernel, steps = packed_utility_kernel, NY
        side = at[:, None, :]
        spec = whole(side)
        scratch = [pltpu.VMEM((NY, at.shape[1], EMB), BF)] + scratch
    return pl.pallas_call(
        kernel,
        grid=(steps,),
        in_specs=[whole(x), spec] + [whole(a) for a in small],
        out_specs=pl.BlockSpec((1, MAXS), lambda i: (0, 0)),
        out_shape=jax.ShapeDtypeStruct((1, MAXS), F32),
        scratch_shapes=scratch,
        compiler_params=pltpu.CompilerParams(vmem_limit_bytes=48 << 20),
    )(x, side, *small)


def project_kernel(pieces, where_ref, rows_ref, mate_ref, *refs):
    out_ref, meta_ref, both_ref = refs[-3:]
    c, first = where_ref[1], where_ref[2]
    refs = list(refs)
    for n, h in zip(pieces, (first, 1 - first)):
        o = 0
        for _ in range(n):
            w_ref = refs.pop(0)
            k = w_ref.shape[0]
            both_ref[pl.ds(pl.multiple_of(h * 128 + o, 64), k), :] = w_ref[:, :HB]
            meta_ref[h, 0, o : o + k, :] = w_ref[:, HB:]
            o += k
    for r_ref, e in ((rows_ref, c), (mate_ref, 1 - c)):
        term = lax.dot_general(r_ref[...], both_ref[...], (((1,), (1,)), ((), ())), preferred_element_type=F32)
        for h in range(2):
            for q in range(NY):
                out_ref[h, 0, q, e] = term[q * CT : (q + 1) * CT, h * 128 : (h + 1) * 128].astype(BF)


def project(at, c, rows, mate, ws, into):
    blocks = (2, 1, NY, NC, CT, 128), (2, 1, 128, 128)
    whole = lambda a: pl.BlockSpec(a.shape, lambda i, at: (0, 0))
    old = [] if into is None else list(into)
    flat = [w for pair in ws for w in pair]
    n = 3 + len(flat)
    return pl.pallas_call(
        functools.partial(project_kernel, [len(pair) for pair in ws]),
        grid_spec=pltpu.PrefetchScalarGridSpec(
            num_scalar_prefetch=1,
            grid=(1,),
            in_specs=[whole(a) for a in (rows, mate, *flat)] + [pl.BlockSpec(memory_space=pl.ANY) for _ in old],
            out_specs=[pl.BlockSpec(b, lambda i, at, d=len(b): (0, at[0]) + (0,) * (d - 2)) for b in blocks],
            scratch_shapes=[pltpu.VMEM((256, HB), BF)],
        ),
        out_shape=[jax.ShapeDtypeStruct((2, 2) + b[2:], BF) for b in blocks],
        input_output_aliases={n: 0, n + 1: 1} if old else {},
        compiler_params=pltpu.CompilerParams(vmem_limit_bytes=40 << 20),
        cost_estimate=pl.CostEstimate(flops=2 * NC * NY * CT * HB * 256, transcendentals=0, bytes_accessed=8 << 20),
    )(jnp.stack([at % 2, c, at // 2]).astype(I32), rows, mate, *flat, *old)


def sum_pack_kernel(x_ref, at_ref, out_ref, v_ref):
    i = pl.program_id(0)
    some, room = out_ref.shape[:2]

    @pl.when(i == 0)
    def _():
        for g in range(NX):
            for e in range(NC):
                v = x_ref[g * NY, e].astype(F32)
                for q in range(1, NY):
                    v = v + x_ref[g * NY + q, e].astype(F32)
                n = g * NC + e
                v_ref[n * CT : (n + 1) * CT, :] = v.astype(BF)

    for b in range(some):
        slot = lax.broadcasted_iota(I32, (room, NX * NC * CT), 0) + (i * some + b) * FAR
        pick = jnp.where(slot == at_ref[...], 1.0, 0.0).astype(BF)
        out_ref[b] = jnp.dot(pick, v_ref[...], preferred_element_type=F32).astype(BF)


def sum_pack(x, at, room):
    n = NX * NC * CT
    some = 4
    return pl.pallas_call(
        sum_pack_kernel,
        grid=(NZ // some,),
        in_specs=[pl.BlockSpec(x.shape, lambda i: (0, 0, 0, 0)), pl.BlockSpec((1, n), lambda i: (0, 0))],
        out_specs=pl.BlockSpec((some, room, 128), lambda i: (i, 0, 0)),
        out_shape=jax.ShapeDtypeStruct((NZ, room, 128), BF),
        scratch_shapes=[pltpu.VMEM((n, 128), BF)],
        compiler_params=pltpu.CompilerParams(vmem_limit_bytes=40 << 20),
    )(x, at.reshape(1, n))


def repack_kernel(x_ref, at_ref, out_ref):
    i = pl.program_id(0)
    some, _, room = out_ref.shape[:3]
    for b in range(some):
        slot = lax.broadcasted_iota(I32, (room, x_ref.shape[0]), 0) + (i * some + b) * FAR
        pick = jnp.where(slot == at_ref[...], 1.0, 0.0).astype(BF)
        v = jnp.dot(pick, x_ref[...], preferred_element_type=F32).astype(BF)
        for q in range(NY):
            out_ref[b, q] = v


def repack(x, at, room):
    n = x.shape[0] * x.shape[1]
    some = 2
    return pl.pallas_call(
        repack_kernel,
        grid=(NX * NC // some,),
        in_specs=[pl.BlockSpec((n, 128), lambda i: (0, 0)), pl.BlockSpec((1, n), lambda i: (0, 0))],
        out_specs=pl.BlockSpec((some, NY, room, 128), lambda i: (i, 0, 0, 0)),
        out_shape=jax.ShapeDtypeStruct((NX * NC, NY, room, 128), BF),
        compiler_params=pltpu.CompilerParams(vmem_limit_bytes=40 << 20),
    )(x.reshape(n, 128), at.reshape(1, n))


def before(n):
    i = jnp.arange(n, dtype=I32)
    return i[:, None] < i[None, :]


def prefix(v):
    return jnp.dot(v.astype(BF), before(v.shape[-1]).astype(BF), preferred_element_type=F32).astype(I32)


def uncompacted(x, y, rows, chunks, dest, all_dest, member):
    rank, member_len, member_weight = member
    projected = jnp.zeros((NX, SEQ * SLOTS, NC * 128), BF)
    c = lax.axis_index("c")
    for k, chunk in zip(RING, chunks[:3] + [jnp.concatenate(chunks[3:])]):
        other = swap(chunk, "c", NC, 1)
        both = jnp.concatenate([jnp.where(c == 1, other, chunk), jnp.where(c == 1, chunk, other)])
        term = lax.dot_general(rows, both[:, :HB], (((1,), (1,)), ((), ())), preferred_element_type=F32)
        projected = lax.dynamic_update_slice(projected, term.astype(BF)[None], ((x + k) % NX, 0, 0))

    by_pos = projected.reshape(NX, NY, POS * SLOTS, NC * 128)
    total = lax.dynamic_index_in_dim(by_pos, y, 1, keepdims=False).astype(F32)
    for k in (1, 3, 2):
        piece = lax.dynamic_index_in_dim(by_pos, (y + k) % NY, 1, keepdims=False)
        total = total + shift(piece, "y", NY, k).astype(F32)
    emb = total.astype(BF).transpose(1, 0, 2).reshape(POS * SLOTS, EMB)

    out_row = jnp.arange(GEN * POS, dtype=I32)
    in_row = jnp.arange(POS, dtype=I32)[:, None] + dest[None, :] * POS
    pick = (out_row[:, None] == in_row.reshape(1, -1)).astype(BF)
    send = jnp.dot(pick, emb, preferred_element_type=F32).astype(BF).reshape(GEN, POS, EMB)
    arrived = lax.all_to_all(send, ("z", "x", "c"), split_axis=0, concat_axis=0, tiled=True)
    src_at = jnp.where(rank[:, None] >= 0, jnp.arange(POS, dtype=I32)[None, :] * MAXS + rank[:, None], -1)
    pick = (jnp.arange(POS * MAXS, dtype=I32)[:, None] == src_at.reshape(1, -1)).astype(BF)
    mine = jnp.dot(pick, arrived.reshape(GEN * POS, EMB), preferred_element_type=F32).astype(BF)

    tokens = jnp.concatenate(two_way_ring(mine, "y", NY))
    pos = jnp.concatenate([((y + k) % NY) * POS + jnp.arange(POS, dtype=I32) for k in RING])
    return utility(tokens, pos[:, None] < member_len[None, :], member_len, member_weight)


def body(hidden, w_proj, slot_prompt, lengths, weights, owner):
    z, x, c, y = (lax.axis_index(a) for a in ("z", "x", "c", "y"))
    me = (z * NX + x) * NC + c
    gens = jnp.arange(GEN, dtype=I32)
    dest = jnp.sum(jnp.where(slot_prompt[:, None] == gens[None, :], owner[None, :], 0), axis=1)

    rows = hidden.reshape(SEQ * SLOTS, HB)
    start = jnp.sum(jnp.where(before(SLOTS), lengths[:, None], 0), axis=0)
    t = jnp.arange(SEQ, dtype=I32)[:, None]
    at = t + start[None, :]
    at = jnp.where(t < lengths[None, :], (at % NY) * CT + at // NY, -1)
    at = jnp.where(start[None, :] + t < NY * CT, at, -1)
    pick = (jnp.arange(NY * CT, dtype=I32)[:, None] == at.reshape(1, -1)).astype(BF)

    meta = jnp.concatenate([dest.astype(BF), lengths.astype(BF), weights, jnp.zeros((32,), BF)])
    part = jnp.concatenate([w_proj.T, jnp.broadcast_to(meta[None, :], (8, 128))], axis=1)
    part = lax.all_gather(part, "z", axis=0, tiled=True)
    pick, part = lax.optimization_barrier((pick, part))
    chunks = two_way_ring(part, "x", NX)
    packed = jnp.dot(pick, rows, preferred_element_type=F32).astype(BF)
    own, prev, after, low, high = chunks
    packed, prev = lax.optimization_barrier((packed, prev))
    mate = swap(packed, "c", NC, 1)
    made = project((x + NX - 1) % NX, c, packed, mate, ((prev,), (after,)), None)
    send, metas = project(x, c, packed, mate, ((own,), (low, high)), made)
    summands = lax.all_to_all(
        send.reshape(NX * NY, NC, CT, 128), ("x", "y"), split_axis=0, concat_axis=0, tiled=True
    )

    metas = metas.reshape(NX, NZ, 8, 128)[:, :, 0]
    twin = swap(metas, "c", NC, 1)
    metas = jnp.stack([jnp.where(c == 1, twin, metas), jnp.where(c == 1, metas, twin)], axis=2)
    metas = metas.transpose(1, 0, 2, 3).reshape(GEN, 128)
    all_dest = metas[:, :32].astype(I32)
    all_len = metas[:, 32:64].astype(I32)
    all_weight = metas[:, 64:96].astype(F32)
    off = prefix(all_len)

    hit = all_dest == me
    present = jnp.any(hit, axis=1)
    rank = jnp.sum((present[:, None] & before(GEN)).astype(I32), axis=0)
    rank = jnp.where(present, rank, -1)
    is_member = jnp.arange(MAXS, dtype=I32)[:, None] == rank[None, :]
    of_member = lambda v, zero: jnp.sum(
        jnp.where(is_member, jnp.sum(jnp.where(hit, v, zero), axis=1)[None, :], zero), axis=1
    )
    member_len, member_off, member_weight = of_member(all_len, 0), of_member(off, 0), of_member(all_weight, 0.0)

    ys = jnp.arange(NY, dtype=I32)[:, None, None]
    on_row = (((off + all_len)[None] + 3 - ys) >> 2) - ((off[None] + 3 - ys) >> 2)
    on_row = on_row.reshape(NY, NZ, NX * NC * SLOTS)
    goes = (all_dest.reshape(NZ, -1)[:, :, None] == gens[None, None, :]).astype(BF)
    load = jnp.einsum("yza,zad->yzd", on_row.astype(BF), goes, preferred_element_type=F32)
    most_along = jnp.max(jnp.sum(load.reshape(NY, NZ, NZ, NX * NC), axis=3))
    most_owned = jnp.max(jnp.sum(load, axis=1))
    fits = jnp.max(off[:, -1] + all_len[:, -1]) <= NY * CT
    choice = sum(jnp.where(fits & (most_along <= a) & (most_owned <= b), 0, 1) for a, b in ROOM)

    lo = (off + 3 - y) >> 2
    hi = (off + all_len + 3 - y) >> 2
    flat = lambda v: v.reshape(NZ, NX * NC * SLOTS)
    n, dz, do = flat(hi - lo), flat(all_dest) // (NX * NC), flat(all_dest) % (NX * NC)
    here = lambda v: lax.dynamic_index_in_dim(v, z, 0, keepdims=False)
    n0, d0 = here(n), here(dz)
    base = jnp.sum(jnp.where(before(n0.shape[0]) & (d0[:, None] == d0[None, :]), n0[:, None], 0), axis=0)
    add = (d0 * FAR + base - here(flat(lo))).reshape(NX * NC, SLOTS, 1)
    j = jnp.arange(CT, dtype=I32)[None, None, :]
    lo0, hi0 = (here(v.reshape(NZ, NX * NC, SLOTS))[:, :, None] for v in (lo, hi))
    at1 = jnp.sum(jnp.where((j >= lo0) & (j < hi0), add + j + 1, 0), axis=1) - 1
    n1 = jnp.where(dz == z, n, 0)
    base1 = prefix(n1)
    o = jnp.arange(NX * NC, dtype=I32)[None, :, None]
    by_owner = jnp.where(do[:, None, :] == o, n1[:, None, :], 0)
    earlier = jnp.sum(jnp.where(before(NZ)[:, :, None], jnp.sum(by_owner, axis=2)[:, None, :], 0), axis=0)
    base2 = prefix(by_owner) + earlier[:, :, None]
    base2 = jnp.sum(jnp.where(do[:, None, :] == o, base2, 0), axis=1)
    add = (do * FAR + base2 - base1)[:, :, None]
    k = jnp.arange(KT, dtype=I32)[None, None, :]
    inside = (k >= base1[:, :, None]) & (k < (base1 + n1)[:, :, None])
    at2 = jnp.sum(jnp.where(inside, add + k + 1, 0), axis=1) - 1
    yy = ys[:, :, 0]
    nm = ((member_off + member_len)[None] + 3 - yy) // 4 - (member_off[None] + 3 - yy) // 4
    basem = prefix(nm)[:, :, None]
    k = jnp.arange(KO, dtype=I32)[None, None, :]
    m = jnp.arange(MAXS, dtype=I32)[None, :, None]
    inside = (k >= basem) & (k < basem + nm[:, :, None])
    at3 = jnp.sum(jnp.where(inside, (k - basem) * MAXS + m + 1, 0), axis=1) - 1
    ok = (jnp.arange(POS, dtype=I32)[None, :, None] < nm[:, None, :]).reshape(SEQ, MAXS)

    def compacted(kt, ko):
        along = lax.all_to_all(sum_pack(summands, at1, kt), "z", split_axis=0, concat_axis=0, tiled=True)
        parts = repack(along, at2[:, :kt], ko).reshape(NX * NC * NY, ko, 128)
        tokens = lax.all_to_all(parts, ("x", "c", "y"), split_axis=0, concat_axis=0, tiled=True)
        return utility(tokens, ok, member_len, member_weight, at3[:, :ko])

    def as_they_are():
        return uncompacted(x, y, rows, chunks, dest, all_dest, (rank, member_len, member_weight))

    return lax.switch(choice, [functools.partial(compacted, *r) for r in ROOM] + [as_they_are])


def solution(mesh):
    fine = Mesh(mesh.devices.reshape(NZ, NX, NC, NY), ("z", "x", "c", "y"))
    g = ("z", "x", "c")
    placed = (P(None, g, "y"), P("y", g), P(g), P(g), P(g), P())
    return jax.shard_map(body, mesh=fine, in_specs=placed, out_specs=P(g, None), check_vma=False)
```

```python
import functools
import math

import jax
import jax.numpy as jnp
from jax import lax
from jax.experimental import pallas as pl
from jax.experimental.pallas import tpu as pltpu
from jax.sharding import Mesh
from jax.sharding import PartitionSpec as P

MAXS = 64
SEQ = 32
EMB = 1024
NZ, NX, NC, NY = 16, 4, 2, 4
GEN = NZ * NX * NC
SLOTS = 32
HB = 2048
BF = jnp.bfloat16
F32 = jnp.float32
I32 = jnp.int32
POS = SEQ // NY
CT = 192
ROOM = ((144, 320), (160, 320), (208, 352))
KT, KO = ROOM[-1]
FAR = 1024


def shift(v, axis, n, k):
    return lax.ppermute(v, axis, [(i, (i + k) % n) for i in range(n)])


def swap(v, axis, n, d):
    return lax.ppermute(v, axis, [(i, i ^ d) for i in range(n)])


def two_way_ring(v, axis, n):
    half = v.shape[0] // 2
    before = shift(v, axis, n, 1)
    after = shift(v, axis, n, n - 1)
    low = shift(before[:half], axis, n, 1)
    high = shift(after[half:], axis, n, n - 1)
    return [v, before, after, low, high]


RING = (0, NY - 1, 1, 2)


def best_match(rows, cols_ref, col_ref):
    best = jnp.full((rows.shape[0], 128), -2.0, F32)
    for q in range(4):
        cols = cols_ref[q * 512 : (q + 1) * 512, :]
        s = lax.dot_general(rows, cols, (((1,), (1,)), ((), ())), preferred_element_type=F32)
        for k in range(4):
            ok = col_ref[q * 4 + k : q * 4 + k + 1, :] > 0
            best = jnp.maximum(best, jnp.where(ok, s[:, k * 128 : (k + 1) * 128], -2.0))
    return jnp.maximum(best[:, :MAXS], best[:, MAXS:])


def finish(acc_ref, live_ref, len_ref, w_ref, out_ref):
    recall = acc_ref[...] / jnp.maximum(len_ref[...], 1.0)
    score = 0.5 * (recall + recall.T)
    util = jnp.sum(score * w_ref[...], axis=0, keepdims=True) / jnp.sum(w_ref[...])
    out_ref[...] = jnp.where(live_ref[...] > 0, util, 0.0)


def unit(v):
    s = lax.rsqrt(jnp.sum(v * v, axis=1, keepdims=True) * (1.0 / EMB) + 1e-6) * (1.0 / math.sqrt(EMB))
    return (v * s).astype(BF)


def utility_kernel(x_ref, row_ref, col_ref, live_ref, len_ref, w_ref, out_ref, xn_ref, acc_ref):
    i = pl.program_id(0)
    blk = row_ref.shape[0]

    @pl.when(i == 0)
    def _():
        acc_ref[...] = jnp.zeros_like(acc_ref)

        def norm(b, carry):
            at = pl.ds(pl.multiple_of(b * blk, blk), blk)
            xn_ref[at, :] = unit(x_ref[at, :].astype(F32))
            return carry

        lax.fori_loop(0, SEQ * MAXS // blk, norm, 0)

    best = best_match(xn_ref[pl.ds(pl.multiple_of(i * blk, blk), blk), :], xn_ref, col_ref)
    best = jnp.where(row_ref[...] > 0, best, 0.0)
    acc_ref[...] += jnp.sum(best.reshape(blk // MAXS, MAXS, MAXS), axis=0)

    @pl.when(i == pl.num_programs(0) - 1)
    def _():
        finish(acc_ref, live_ref, len_ref, w_ref, out_ref)


def packed_utility_kernel(x_ref, at_ref, col_ref, live_ref, len_ref, w_ref, out_ref, rows_ref, cols_ref, acc_ref):
    i = pl.program_id(0)
    room = at_ref.shape[2]

    @pl.when(i == 0)
    def _():
        acc_ref[...] = jnp.zeros_like(acc_ref)
        for q in range(NY):
            v = jnp.concatenate([x_ref[g * NY + q] for g in range(NX * NC)], axis=1)
            v = unit(v.astype(F32))
            rows_ref[q] = v
            slot = lax.broadcasted_iota(I32, (POS * MAXS, room), 0)
            pick = jnp.where(slot == at_ref[q], 1.0, 0.0).astype(BF)
            v = jnp.dot(pick, v, preferred_element_type=F32)
            cols_ref[q * POS * MAXS : (q + 1) * POS * MAXS, :] = v.astype(BF)

    best = best_match(rows_ref[i], cols_ref, col_ref)
    at = at_ref[i]
    mine = (lax.broadcasted_iota(I32, (MAXS, room), 0) == at % MAXS) & (at >= 0)
    acc_ref[...] += jnp.dot(
        jnp.where(mine, 1.0, 0.0), best, precision=lax.Precision.HIGHEST, preferred_element_type=F32
    )

    @pl.when(i == pl.num_programs(0) - 1)
    def _():
        finish(acc_ref, live_ref, len_ref, w_ref, out_ref)


def utility(x, ok, member_len, member_weight, at=None):
    n = SEQ * MAXS
    whole = lambda a: pl.BlockSpec(a.shape, lambda i, d=a.ndim: (0,) * d)
    live = (member_len > 0).astype(F32)[None, :]
    small = [ok.astype(F32).reshape(n // 128, 128), live, member_len.astype(F32)[:, None], member_weight[:, None]]
    scratch = [pltpu.VMEM((n, EMB), BF), pltpu.VMEM((MAXS, MAXS), F32)]
    if at is None:
        kernel, steps = utility_kernel, 8
        side, spec = ok.astype(F32).reshape(n, 1), pl.BlockSpec((n // steps, 1), lambda i: (i, 0))
    else:
        kernel, steps = packed_utility_kernel, NY
        side = at[:, None, :]
        spec = whole(side)
        scratch = [pltpu.VMEM((NY, at.shape[1], EMB), BF)] + scratch
    return pl.pallas_call(
        kernel,
        grid=(steps,),
        in_specs=[whole(x), spec] + [whole(a) for a in small],
        out_specs=pl.BlockSpec((1, MAXS), lambda i: (0, 0)),
        out_shape=jax.ShapeDtypeStruct((1, MAXS), F32),
        scratch_shapes=scratch,
        compiler_params=pltpu.CompilerParams(vmem_limit_bytes=48 << 20),
    )(x, side, *small)


def with_meta_kernel(w_ref, prompt_ref, len_ref, weight_ref, out_ref):
    out_ref[:, :HB] = w_ref[...]
    row = lax.broadcasted_iota(I32, (8, SLOTS), 0)
    v = jnp.where(row == 0, prompt_ref[...].astype(F32), jnp.where(row == 1, len_ref[...].astype(F32), 0.0))
    v = jnp.where(row == 2, weight_ref[...].astype(F32), v)
    out_ref[:, HB:] = jnp.concatenate([v, jnp.zeros((8, 128 - SLOTS), F32)], axis=1).astype(BF)


def with_meta(w, prompt, length, weight):
    return pl.pallas_call(with_meta_kernel, out_shape=jax.ShapeDtypeStruct((8, HB + 128), BF))(
        w, prompt[None, :], length[None, :], weight[None, :]
    )


def project_kernel(pieces, where_ref, rows_ref, mate_ref, *refs):
    out_ref, meta_ref, both_ref = refs[-3:]
    c, first = where_ref[1], where_ref[2]
    refs = list(refs)
    for n, h in zip(pieces, (first, 1 - first)):
        o = 0
        for _ in range(n):
            w_ref = refs.pop(0)
            k = w_ref.shape[0]
            both_ref[pl.ds(pl.multiple_of(h * 128 + o, 64), k), :] = w_ref[:, :HB]
            meta_ref[h, 0, o : o + k, :] = w_ref[:, HB:]
            o += k
    for r_ref, e in ((rows_ref, c), (mate_ref, 1 - c)):
        term = lax.dot_general(r_ref[...], both_ref[...], (((1,), (1,)), ((), ())), preferred_element_type=F32)
        for h in range(2):
            for q in range(NY):
                out_ref[h, 0, q, e] = term[q * CT : (q + 1) * CT, h * 128 : (h + 1) * 128].astype(BF)


def project(at, c, rows, mate, ws, into):
    blocks = (2, 1, NY, NC, CT, 128), (2, 1, 128, 128)
    whole = lambda a: pl.BlockSpec(a.shape, lambda i, at: (0, 0))
    old = [] if into is None else list(into)
    flat = [w for pair in ws for w in pair]
    n = 3 + len(flat)
    return pl.pallas_call(
        functools.partial(project_kernel, [len(pair) for pair in ws]),
        grid_spec=pltpu.PrefetchScalarGridSpec(
            num_scalar_prefetch=1,
            grid=(1,),
            in_specs=[whole(a) for a in (rows, mate, *flat)] + [pl.BlockSpec(memory_space=pl.ANY) for _ in old],
            out_specs=[pl.BlockSpec(b, lambda i, at, d=len(b): (0, at[0]) + (0,) * (d - 2)) for b in blocks],
            scratch_shapes=[pltpu.VMEM((256, HB), BF)],
        ),
        out_shape=[jax.ShapeDtypeStruct((2, 2) + b[2:], BF) for b in blocks],
        input_output_aliases={n: 0, n + 1: 1} if old else {},
        compiler_params=pltpu.CompilerParams(vmem_limit_bytes=40 << 20),
        cost_estimate=pl.CostEstimate(flops=2 * NC * NY * CT * HB * 256, transcendentals=0, bytes_accessed=8 << 20),
    )(jnp.stack([at % 2, c, at // 2]).astype(I32), rows, mate, *flat, *old)


def sum_pack_kernel(x_ref, at_ref, out_ref, v_ref):
    i = pl.program_id(0)
    some, room = out_ref.shape[:2]

    @pl.when(i == 0)
    def _():
        for g in range(NX):
            for e in range(NC):
                v = x_ref[g * NY, e].astype(F32)
                for q in range(1, NY):
                    v = v + x_ref[g * NY + q, e].astype(F32)
                n = g * NC + e
                v_ref[n * CT : (n + 1) * CT, :] = v.astype(BF)

    for b in range(some):
        slot = lax.broadcasted_iota(I32, (room, NX * NC * CT), 0) + (i * some + b) * FAR
        pick = jnp.where(slot == at_ref[...], 1.0, 0.0).astype(BF)
        out_ref[b] = jnp.dot(pick, v_ref[...], preferred_element_type=F32).astype(BF)


def sum_pack(x, at, room):
    n = NX * NC * CT
    some = 4
    return pl.pallas_call(
        sum_pack_kernel,
        grid=(NZ // some,),
        in_specs=[pl.BlockSpec(x.shape, lambda i: (0, 0, 0, 0)), pl.BlockSpec((1, n), lambda i: (0, 0))],
        out_specs=pl.BlockSpec((some, room, 128), lambda i: (i, 0, 0)),
        out_shape=jax.ShapeDtypeStruct((NZ, room, 128), BF),
        scratch_shapes=[pltpu.VMEM((n, 128), BF)],
        compiler_params=pltpu.CompilerParams(vmem_limit_bytes=40 << 20),
    )(x, at.reshape(1, n))


def repack_kernel(x_ref, at_ref, out_ref):
    i = pl.program_id(0)
    some, _, room = out_ref.shape[:3]
    for b in range(some):
        slot = lax.broadcasted_iota(I32, (room, x_ref.shape[0]), 0) + (i * some + b) * FAR
        pick = jnp.where(slot == at_ref[...], 1.0, 0.0).astype(BF)
        v = jnp.dot(pick, x_ref[...], preferred_element_type=F32).astype(BF)
        for q in range(NY):
            out_ref[b, q] = v


def repack(x, at, room):
    n = x.shape[0] * x.shape[1]
    some = 2
    return pl.pallas_call(
        repack_kernel,
        grid=(NX * NC // some,),
        in_specs=[pl.BlockSpec((n, 128), lambda i: (0, 0)), pl.BlockSpec((1, n), lambda i: (0, 0))],
        out_specs=pl.BlockSpec((some, NY, room, 128), lambda i: (i, 0, 0, 0)),
        out_shape=jax.ShapeDtypeStruct((NX * NC, NY, room, 128), BF),
        compiler_params=pltpu.CompilerParams(vmem_limit_bytes=40 << 20),
    )(x.reshape(n, 128), at.reshape(1, n))


def before(n):
    i = jnp.arange(n, dtype=I32)
    return i[:, None] < i[None, :]


def prefix(v):
    return jnp.dot(v.astype(BF), before(v.shape[-1]).astype(BF), preferred_element_type=F32).astype(I32)


def uncompacted(x, y, rows, chunks, dest, all_dest, member):
    rank, member_len, member_weight = member
    projected = jnp.zeros((NX, SEQ * SLOTS, NC * 128), BF)
    c = lax.axis_index("c")
    for k, chunk in zip(RING, chunks[:3] + [jnp.concatenate(chunks[3:])]):
        other = swap(chunk, "c", NC, 1)
        both = jnp.concatenate([jnp.where(c == 1, other, chunk), jnp.where(c == 1, chunk, other)])
        term = lax.dot_general(rows, both[:, :HB], (((1,), (1,)), ((), ())), preferred_element_type=F32)
        projected = lax.dynamic_update_slice(projected, term.astype(BF)[None], ((x + k) % NX, 0, 0))

    by_pos = projected.reshape(NX, NY, POS * SLOTS, NC * 128)
    total = lax.dynamic_index_in_dim(by_pos, y, 1, keepdims=False).astype(F32)
    for k in (1, 3, 2):
        piece = lax.dynamic_index_in_dim(by_pos, (y + k) % NY, 1, keepdims=False)
        total = total + shift(piece, "y", NY, k).astype(F32)
    emb = total.astype(BF).transpose(1, 0, 2).reshape(POS * SLOTS, EMB)

    out_row = jnp.arange(GEN * POS, dtype=I32)
    in_row = jnp.arange(POS, dtype=I32)[:, None] + dest[None, :] * POS
    pick = (out_row[:, None] == in_row.reshape(1, -1)).astype(BF)
    send = jnp.dot(pick, emb, preferred_element_type=F32).astype(BF).reshape(GEN, POS, EMB)
    arrived = lax.all_to_all(send, ("z", "x", "c"), split_axis=0, concat_axis=0, tiled=True)
    src_at = jnp.where(rank[:, None] >= 0, jnp.arange(POS, dtype=I32)[None, :] * MAXS + rank[:, None], -1)
    pick = (jnp.arange(POS * MAXS, dtype=I32)[:, None] == src_at.reshape(1, -1)).astype(BF)
    mine = jnp.dot(pick, arrived.reshape(GEN * POS, EMB), preferred_element_type=F32).astype(BF)

    tokens = jnp.concatenate(two_way_ring(mine, "y", NY))
    pos = jnp.concatenate([((y + k) % NY) * POS + jnp.arange(POS, dtype=I32) for k in RING])
    return utility(tokens, pos[:, None] < member_len[None, :], member_len, member_weight)


def body(hidden, w_proj, slot_prompt, lengths, weights, owner):
    z, x, c, y = (lax.axis_index(a) for a in ("z", "x", "c", "y"))
    me = (z * NX + x) * NC + c
    gens = jnp.arange(GEN, dtype=I32)

    part = with_meta(w_proj.T, slot_prompt, lengths, weights)
    part = lax.all_gather(part, "z", axis=0, tiled=True)
    lens, part = lax.optimization_barrier((lengths, part))

    rows = hidden.reshape(SEQ * SLOTS, HB)
    start = jnp.sum(jnp.where(before(SLOTS), lens[:, None], 0), axis=0)
    t = jnp.arange(SEQ, dtype=I32)[:, None]
    at = t + start[None, :]
    at = jnp.where((t < lens[None, :]) & (at < NY * CT), (at % NY) * CT + at // NY, -1)
    pick = (jnp.arange(NY * CT, dtype=I32)[:, None] == at.reshape(1, -1)).astype(BF)
    chunks = two_way_ring(part, "x", NX)
    packed = jnp.dot(pick, rows, preferred_element_type=F32).astype(BF)
    own, prev, after, low, high = chunks
    packed, prev, after = lax.optimization_barrier((packed, prev, after))
    mate = swap(packed, "c", NC, 1)
    made = project((x + NX - 1) % NX, c, packed, mate, ((prev,), (after,)), None)
    send, metas = project(x, c, packed, mate, ((own,), (low, high)), made)
    summands = lax.all_to_all(
        send.reshape(NX * NY, NC, CT, 128), ("x", "y"), split_axis=0, concat_axis=0, tiled=True
    )

    metas = metas.reshape(NX, NZ, 8, 128)[:, :, :3]
    twin = swap(metas, "c", NC, 1)
    metas = jnp.stack([jnp.where(c == 1, twin, metas), jnp.where(c == 1, metas, twin)], axis=2)
    metas = metas.transpose(3, 1, 0, 2, 4).reshape(3, GEN, 128)[:, :, :SLOTS]
    all_prompt = metas[0].astype(I32)
    all_len = metas[1].astype(I32)
    all_weight = metas[2].astype(F32)
    all_dest = jnp.sum(jnp.where(all_prompt[:, :, None] == gens, owner, 0), axis=2)
    off = prefix(all_len)

    hit = all_dest == me
    present = jnp.any(hit, axis=1)
    rank = jnp.sum((present[:, None] & before(GEN)).astype(I32), axis=0)
    rank = jnp.where(present, rank, -1)
    is_member = jnp.arange(MAXS, dtype=I32)[:, None] == rank[None, :]
    of_member = lambda v, zero: jnp.sum(
        jnp.where(is_member, jnp.sum(jnp.where(hit, v, zero), axis=1)[None, :], zero), axis=1
    )
    member_len, member_off, member_weight = of_member(all_len, 0), of_member(off, 0), of_member(all_weight, 0.0)

    ys = jnp.arange(NY, dtype=I32)[:, None, None]
    on_row = (((off + all_len)[None] + 3 - ys) >> 2) - ((off[None] + 3 - ys) >> 2)
    on_row = on_row.reshape(NY, NZ, NX * NC * SLOTS)
    goes = (all_dest.reshape(NZ, -1)[:, :, None] == gens[None, None, :]).astype(BF)
    load = jnp.einsum("yza,zad->yzd", on_row.astype(BF), goes, preferred_element_type=F32)
    most_along = jnp.max(jnp.sum(load.reshape(NY, NZ, NZ, NX * NC), axis=3))
    most_owned = jnp.max(jnp.sum(load, axis=1))
    fits = jnp.max(off[:, -1] + all_len[:, -1]) <= NY * CT
    choice = sum(jnp.where(fits & (most_along <= a) & (most_owned <= b), 0, 1) for a, b in ROOM)

    lo = (off + 3 - y) >> 2
    hi = (off + all_len + 3 - y) >> 2
    flat = lambda v: v.reshape(NZ, NX * NC * SLOTS)
    n, dz, do = flat(hi - lo), flat(all_dest) // (NX * NC), flat(all_dest) % (NX * NC)
    here = lambda v: lax.dynamic_index_in_dim(v, z, 0, keepdims=False)
    n0, d0 = here(n), here(dz)
    base = jnp.sum(jnp.where(before(n0.shape[0]) & (d0[:, None] == d0[None, :]), n0[:, None], 0), axis=0)
    add = (d0 * FAR + base - here(flat(lo))).reshape(NX * NC, SLOTS, 1)
    j = jnp.arange(CT, dtype=I32)[None, None, :]
    lo0, hi0 = (here(v.reshape(NZ, NX * NC, SLOTS))[:, :, None] for v in (lo, hi))
    at1 = jnp.sum(jnp.where((j >= lo0) & (j < hi0), add + j + 1, 0), axis=1) - 1
    n1 = jnp.where(dz == z, n, 0)
    base1 = prefix(n1)
    o = jnp.arange(NX * NC, dtype=I32)[None, :, None]
    by_owner = jnp.where(do[:, None, :] == o, n1[:, None, :], 0)
    earlier = jnp.sum(jnp.where(before(NZ)[:, :, None], jnp.sum(by_owner, axis=2)[:, None, :], 0), axis=0)
    base2 = prefix(by_owner) + earlier[:, :, None]
    base2 = jnp.sum(jnp.where(do[:, None, :] == o, base2, 0), axis=1)
    add = (do * FAR + base2 - base1)[:, :, None]
    k = jnp.arange(KT, dtype=I32)[None, None, :]
    inside = (k >= base1[:, :, None]) & (k < (base1 + n1)[:, :, None])
    at2 = jnp.sum(jnp.where(inside, add + k + 1, 0), axis=1) - 1
    yy = ys[:, :, 0]
    nm = ((member_off + member_len)[None] + 3 - yy) // 4 - (member_off[None] + 3 - yy) // 4
    basem = prefix(nm)[:, :, None]
    k = jnp.arange(KO, dtype=I32)[None, None, :]
    m = jnp.arange(MAXS, dtype=I32)[None, :, None]
    inside = (k >= basem) & (k < basem + nm[:, :, None])
    at3 = jnp.sum(jnp.where(inside, (k - basem) * MAXS + m + 1, 0), axis=1) - 1
    ok = (jnp.arange(POS, dtype=I32)[None, :, None] < nm[:, None, :]).reshape(SEQ, MAXS)

    def compacted(kt, ko):
        along = lax.all_to_all(sum_pack(summands, at1, kt), "z", split_axis=0, concat_axis=0, tiled=True)
        parts = repack(along, at2[:, :kt], ko).reshape(NX * NC * NY, ko, 128)
        tokens = lax.all_to_all(parts, ("x", "c", "y"), split_axis=0, concat_axis=0, tiled=True)
        return utility(tokens, ok, member_len, member_weight, at3[:, :ko])

    def as_they_are():
        dest = jnp.sum(jnp.where(slot_prompt[:, None] == gens[None, :], owner[None, :], 0), axis=1)
        return uncompacted(x, y, rows, chunks, dest, all_dest, (rank, member_len, member_weight))

    return lax.switch(choice, [functools.partial(compacted, *r) for r in ROOM] + [as_they_are])


def solution(mesh):
    fine = Mesh(mesh.devices.reshape(NZ, NX, NC, NY), ("z", "x", "c", "y"))
    g = ("z", "x", "c")
    placed = (P(None, g, "y"), P("y", g), P(g), P(g), P(g), P())
    return jax.shard_map(body, mesh=fine, in_specs=placed, out_specs=P(g, None), check_vma=False)
```

```python
import functools
import math

import jax
import jax.numpy as jnp
from jax import lax
from jax.experimental import pallas as pl
from jax.experimental.pallas import tpu as pltpu
from jax.sharding import Mesh
from jax.sharding import PartitionSpec as P

MAXS = 64
SEQ = 32
EMB = 1024
NZ, NX, NC, NY = 16, 4, 2, 4
GEN = NZ * NX * NC
SLOTS = 32
HB = 2048
BF = jnp.bfloat16
F32 = jnp.float32
I32 = jnp.int32
POS = SEQ // NY
CT = 192
ROOM = ((160, 320), (208, 352))
KT, KO = ROOM[-1]
FAR = 1024


def shift(v, axis, n, k):
    return lax.ppermute(v, axis, [(i, (i + k) % n) for i in range(n)])


def swap(v, axis, n, d):
    return lax.ppermute(v, axis, [(i, i ^ d) for i in range(n)])


def two_way_ring(v, axis, n):
    half = v.shape[0] // 2
    before = shift(v, axis, n, 1)
    after = shift(v, axis, n, n - 1)
    low = shift(before[:half], axis, n, 1)
    high = shift(after[half:], axis, n, n - 1)
    return [v, before, after, low, high]


RING = (0, NY - 1, 1, 2)


def best_match(rows, cols_ref, col_ref):

    def some(q, best):
        cols = cols_ref[pl.ds(pl.multiple_of(q * 512, 512), 512), :]
        s = lax.dot_general(rows, cols, (((1,), (1,)), ((), ())), preferred_element_type=F32)
        ok = col_ref[q] > 0
        for k in range(4):
            best = jnp.maximum(best, jnp.where(ok[k : k + 1], s[:, k * 128 : (k + 1) * 128], -2.0))
        return best

    best = lax.fori_loop(0, 4, some, jnp.full((rows.shape[0], 128), -2.0, F32))
    return jnp.maximum(best[:, :MAXS], best[:, MAXS:])


def finish(acc_ref, live_ref, len_ref, w_ref, out_ref):
    recall = acc_ref[...] / jnp.maximum(len_ref[...], 1.0)
    score = 0.5 * (recall + recall.T)
    util = jnp.sum(score * w_ref[...], axis=0, keepdims=True) / jnp.sum(w_ref[...])
    out_ref[...] = jnp.where(live_ref[...] > 0, util, 0.0)


def unit(v):
    s = lax.rsqrt(jnp.sum(v * v, axis=1, keepdims=True) * (1.0 / EMB) + 1e-6) * (1.0 / math.sqrt(EMB))
    return (v * s).astype(BF)


def utility_kernel(x_ref, row_ref, col_ref, live_ref, len_ref, w_ref, out_ref, xn_ref, acc_ref):
    i = pl.program_id(0)
    blk = row_ref.shape[0]

    @pl.when(i == 0)
    def _():
        acc_ref[...] = jnp.zeros_like(acc_ref)

        def norm(b, carry):
            at = pl.ds(pl.multiple_of(b * blk, blk), blk)
            xn_ref[at, :] = unit(x_ref[at, :].astype(F32))
            return carry

        lax.fori_loop(0, SEQ * MAXS // blk, norm, 0)

    best = best_match(xn_ref[pl.ds(pl.multiple_of(i * blk, blk), blk), :], xn_ref, col_ref)
    best = jnp.where(row_ref[...] > 0, best, 0.0)
    acc_ref[...] += jnp.sum(best.reshape(blk // MAXS, MAXS, MAXS), axis=0)

    @pl.when(i == pl.num_programs(0) - 1)
    def _():
        finish(acc_ref, live_ref, len_ref, w_ref, out_ref)


def packed_utility_kernel(x_ref, at_ref, col_ref, live_ref, len_ref, w_ref, out_ref, rows_ref, cols_ref, acc_ref):
    i = pl.program_id(0)
    room = at_ref.shape[2]

    @pl.when(i == 0)
    def _():
        acc_ref[...] = jnp.zeros_like(acc_ref)

        def place(q, carry):
            v = jnp.concatenate([x_ref[g * NY + q] for g in range(NX * NC)], axis=1)
            v = unit(v.astype(F32))
            rows_ref[q] = v
            slot = lax.broadcasted_iota(I32, (POS * MAXS, room), 0)
            pick = jnp.where(slot == at_ref[q], 1.0, 0.0).astype(BF)
            v = jnp.dot(pick, v, preferred_element_type=F32)
            cols_ref[pl.ds(pl.multiple_of(q * POS * MAXS, 512), POS * MAXS), :] = v.astype(BF)
            return carry

        lax.fori_loop(0, NY, place, 0)

    best = best_match(rows_ref[i], cols_ref, col_ref)
    at = at_ref[i]
    mine = (lax.broadcasted_iota(I32, (MAXS, room), 0) == at % MAXS) & (at >= 0)
    acc_ref[...] += jnp.dot(
        jnp.where(mine, 1.0, 0.0), best, precision=lax.Precision.HIGHEST, preferred_element_type=F32
    )

    @pl.when(i == pl.num_programs(0) - 1)
    def _():
        finish(acc_ref, live_ref, len_ref, w_ref, out_ref)


def utility(x, ok, member_len, member_weight, at=None):
    n = SEQ * MAXS
    whole = lambda a: pl.BlockSpec(a.shape, lambda i, d=a.ndim: (0,) * d)
    live = (member_len > 0).astype(F32)[None, :]
    small = [ok.astype(F32).reshape(4, n // 512, 128), live, member_len.astype(F32)[:, None], member_weight[:, None]]
    scratch = [pltpu.VMEM((n, EMB), BF), pltpu.VMEM((MAXS, MAXS), F32)]
    if at is None:
        kernel, steps = utility_kernel, 8
        side, spec = ok.astype(F32).reshape(n, 1), pl.BlockSpec((n // steps, 1), lambda i: (i, 0))
    else:
        kernel, steps = packed_utility_kernel, NY
        side = at[:, None, :]
        spec = whole(side)
        scratch = [pltpu.VMEM((NY, at.shape[1], EMB), BF)] + scratch
    return pl.pallas_call(
        kernel,
        grid=(steps,),
        in_specs=[whole(x), spec] + [whole(a) for a in small],
        out_specs=pl.BlockSpec((1, MAXS), lambda i: (0, 0)),
        out_shape=jax.ShapeDtypeStruct((1, MAXS), F32),
        scratch_shapes=scratch,
        compiler_params=pltpu.CompilerParams(vmem_limit_bytes=48 << 20),
    )(x, side, *small)


def with_meta_kernel(w_ref, prompt_ref, len_ref, weight_ref, out_ref):
    out_ref[:, :HB] = w_ref[...]
    row = lax.broadcasted_iota(I32, (8, SLOTS), 0)
    v = jnp.where(row == 0, prompt_ref[...].astype(F32), jnp.where(row == 1, len_ref[...].astype(F32), 0.0))
    v = jnp.where(row == 2, weight_ref[...].astype(F32), v)
    out_ref[:, HB:] = jnp.concatenate([v, jnp.zeros((8, 128 - SLOTS), F32)], axis=1).astype(BF)


def with_meta(w, prompt, length, weight):
    return pl.pallas_call(with_meta_kernel, out_shape=jax.ShapeDtypeStruct((8, HB + 128), BF))(
        w, prompt[None, :], length[None, :], weight[None, :]
    )


def project_kernel(pieces, where_ref, rows_ref, mate_ref, *refs):
    out_ref, meta_ref, both_ref = refs[-3:]
    c, first = where_ref[1], where_ref[2]
    refs = list(refs)
    for n, h in zip(pieces, (first, 1 - first)):
        o = 0
        for _ in range(n):
            w_ref = refs.pop(0)
            k = w_ref.shape[0]
            both_ref[pl.ds(pl.multiple_of(h * 128 + o, 64), k), :] = w_ref[:, :HB]
            meta_ref[h, 0, o : o + k, :] = w_ref[:, HB:]
            o += k
    for r_ref, e in ((rows_ref, c), (mate_ref, 1 - c)):
        term = lax.dot_general(r_ref[...], both_ref[...], (((1,), (1,)), ((), ())), preferred_element_type=F32)
        for h in range(2):
            for q in range(NY):
                out_ref[h, 0, q, e] = term[q * CT : (q + 1) * CT, h * 128 : (h + 1) * 128].astype(BF)


def project(at, c, rows, mate, ws, into):
    blocks = (2, 1, NY, NC, CT, 128), (2, 1, 128, 128)
    whole = lambda a: pl.BlockSpec(a.shape, lambda i, at: (0, 0))
    old = [] if into is None else list(into)
    flat = [w for pair in ws for w in pair]
    n = 3 + len(flat)
    return pl.pallas_call(
        functools.partial(project_kernel, [len(pair) for pair in ws]),
        grid_spec=pltpu.PrefetchScalarGridSpec(
            num_scalar_prefetch=1,
            grid=(1,),
            in_specs=[whole(a) for a in (rows, mate, *flat)] + [pl.BlockSpec(memory_space=pl.ANY) for _ in old],
            out_specs=[pl.BlockSpec(b, lambda i, at, d=len(b): (0, at[0]) + (0,) * (d - 2)) for b in blocks],
            scratch_shapes=[pltpu.VMEM((256, HB), BF)],
        ),
        out_shape=[jax.ShapeDtypeStruct((2, 2) + b[2:], BF) for b in blocks],
        input_output_aliases={n: 0, n + 1: 1} if old else {},
        compiler_params=pltpu.CompilerParams(vmem_limit_bytes=40 << 20),
        cost_estimate=pl.CostEstimate(flops=2 * NC * NY * CT * HB * 256, transcendentals=0, bytes_accessed=8 << 20),
    )(jnp.stack([at % 2, c, at // 2]).astype(I32), rows, mate, *flat, *old)


def sum_pack_kernel(x_ref, at_ref, out_ref, v_ref):
    i = pl.program_id(0)
    some, room = out_ref.shape[:2]

    @pl.when(i == 0)
    def _():

        def add(g, carry):
            for e in range(NC):
                v = x_ref[g * NY, e].astype(F32)
                for q in range(1, NY):
                    v = v + x_ref[g * NY + q, e].astype(F32)
                v_ref[pl.ds(pl.multiple_of((g * NC + e) * CT, 64), CT), :] = v.astype(BF)
            return carry

        lax.fori_loop(0, NX, add, 0)

    def bucket(b, carry):
        slot = lax.broadcasted_iota(I32, (room, NX * NC * CT), 0) + (i * some + b) * FAR
        pick = jnp.where(slot == at_ref[...], 1.0, 0.0).astype(BF)
        out_ref[b] = jnp.dot(pick, v_ref[...], preferred_element_type=F32).astype(BF)
        return carry

    lax.fori_loop(0, some, bucket, 0)


def sum_pack(x, at, room):
    n = NX * NC * CT
    some = 4
    return pl.pallas_call(
        sum_pack_kernel,
        grid=(NZ // some,),
        in_specs=[pl.BlockSpec(x.shape, lambda i: (0, 0, 0, 0)), pl.BlockSpec((1, n), lambda i: (0, 0))],
        out_specs=pl.BlockSpec((some, room, 128), lambda i: (i, 0, 0)),
        out_shape=jax.ShapeDtypeStruct((NZ, room, 128), BF),
        scratch_shapes=[pltpu.VMEM((n, 128), BF)],
        compiler_params=pltpu.CompilerParams(vmem_limit_bytes=40 << 20),
    )(x, at.reshape(1, n))


def repack_kernel(x_ref, at_ref, out_ref):
    i = pl.program_id(0)
    some, _, room = out_ref.shape[:3]

    def owner(b, carry):
        slot = lax.broadcasted_iota(I32, (room, x_ref.shape[0]), 0) + (i * some + b) * FAR
        pick = jnp.where(slot == at_ref[...], 1.0, 0.0).astype(BF)
        v = jnp.dot(pick, x_ref[...], preferred_element_type=F32).astype(BF)
        for q in range(NY):
            out_ref[b, q] = v
        return carry

    lax.fori_loop(0, some, owner, 0)


def repack(x, at, room):
    n = x.shape[0] * x.shape[1]
    some = 2
    return pl.pallas_call(
        repack_kernel,
        grid=(NX * NC // some,),
        in_specs=[pl.BlockSpec((n, 128), lambda i: (0, 0)), pl.BlockSpec((1, n), lambda i: (0, 0))],
        out_specs=pl.BlockSpec((some, NY, room, 128), lambda i: (i, 0, 0, 0)),
        out_shape=jax.ShapeDtypeStruct((NX * NC, NY, room, 128), BF),
        compiler_params=pltpu.CompilerParams(vmem_limit_bytes=40 << 20),
    )(x.reshape(n, 128), at.reshape(1, n))


def before(n):
    i = jnp.arange(n, dtype=I32)
    return i[:, None] < i[None, :]


def prefix(v):
    return jnp.dot(v.astype(BF), before(v.shape[-1]).astype(BF), preferred_element_type=F32).astype(I32)


def uncompacted(x, y, rows, chunks, dest, all_dest, member):
    rank, member_len, member_weight = member
    projected = jnp.zeros((NX, SEQ * SLOTS, NC * 128), BF)
    c = lax.axis_index("c")
    for k, chunk in zip(RING, chunks[:3] + [jnp.concatenate(chunks[3:])]):
        other = swap(chunk, "c", NC, 1)
        both = jnp.concatenate([jnp.where(c == 1, other, chunk), jnp.where(c == 1, chunk, other)])
        term = lax.dot_general(rows, both[:, :HB], (((1,), (1,)), ((), ())), preferred_element_type=F32)
        projected = lax.dynamic_update_slice(projected, term.astype(BF)[None], ((x + k) % NX, 0, 0))

    by_pos = projected.reshape(NX, NY, POS * SLOTS, NC * 128)
    total = lax.dynamic_index_in_dim(by_pos, y, 1, keepdims=False).astype(F32)
    for k in (1, 3, 2):
        piece = lax.dynamic_index_in_dim(by_pos, (y + k) % NY, 1, keepdims=False)
        total = total + shift(piece, "y", NY, k).astype(F32)
    emb = total.astype(BF).transpose(1, 0, 2).reshape(POS * SLOTS, EMB)

    out_row = jnp.arange(GEN * POS, dtype=I32)
    in_row = jnp.arange(POS, dtype=I32)[:, None] + dest[None, :] * POS
    pick = (out_row[:, None] == in_row.reshape(1, -1)).astype(BF)
    send = jnp.dot(pick, emb, preferred_element_type=F32).astype(BF).reshape(GEN, POS, EMB)
    arrived = lax.all_to_all(send, ("z", "x", "c"), split_axis=0, concat_axis=0, tiled=True)
    src_at = jnp.where(rank[:, None] >= 0, jnp.arange(POS, dtype=I32)[None, :] * MAXS + rank[:, None], -1)
    pick = (jnp.arange(POS * MAXS, dtype=I32)[:, None] == src_at.reshape(1, -1)).astype(BF)
    mine = jnp.dot(pick, arrived.reshape(GEN * POS, EMB), preferred_element_type=F32).astype(BF)

    tokens = jnp.concatenate(two_way_ring(mine, "y", NY))
    pos = jnp.concatenate([((y + k) % NY) * POS + jnp.arange(POS, dtype=I32) for k in RING])
    return utility(tokens, pos[:, None] < member_len[None, :], member_len, member_weight)


def body(hidden, w_proj, slot_prompt, lengths, weights, owner):
    z, x, c, y = (lax.axis_index(a) for a in ("z", "x", "c", "y"))
    me = (z * NX + x) * NC + c
    gens = jnp.arange(GEN, dtype=I32)

    part = with_meta(w_proj.T, slot_prompt, lengths, weights)
    part = lax.all_gather(part, "z", axis=0, tiled=True)
    lens, part = lax.optimization_barrier((lengths, part))

    rows = hidden.reshape(SEQ * SLOTS, HB)
    start = jnp.sum(jnp.where(before(SLOTS), lens[:, None], 0), axis=0)
    t = jnp.arange(SEQ, dtype=I32)[:, None]
    at = t + start[None, :]
    at = jnp.where((t < lens[None, :]) & (at < NY * CT), (at % NY) * CT + at // NY, -1)
    pick = (jnp.arange(NY * CT, dtype=I32)[:, None] == at.reshape(1, -1)).astype(BF)
    chunks = two_way_ring(part, "x", NX)
    packed = jnp.dot(pick, rows, preferred_element_type=F32).astype(BF)
    own, prev, after, low, high = chunks
    packed, prev, after = lax.optimization_barrier((packed, prev, after))
    mate = swap(packed, "c", NC, 1)
    made = project((x + NX - 1) % NX, c, packed, mate, ((prev,), (after,)), None)
    send, metas = project(x, c, packed, mate, ((own,), (low, high)), made)
    summands = lax.all_to_all(
        send.reshape(NX * NY, NC, CT, 128), ("x", "y"), split_axis=0, concat_axis=0, tiled=True
    )

    metas = metas.reshape(NX, NZ, 8, 128)[:, :, :3]
    twin = swap(metas, "c", NC, 1)
    metas = jnp.stack([jnp.where(c == 1, twin, metas), jnp.where(c == 1, metas, twin)], axis=2)
    metas = metas.transpose(3, 1, 0, 2, 4).reshape(3, GEN, 128)[:, :, :SLOTS]
    all_prompt = metas[0].astype(I32)
    all_len = metas[1].astype(I32)
    all_weight = metas[2].astype(F32)
    all_dest = jnp.sum(jnp.where(all_prompt[:, :, None] == gens, owner, 0), axis=2)
    off = prefix(all_len)

    hit = all_dest == me
    present = jnp.any(hit, axis=1)
    rank = jnp.sum((present[:, None] & before(GEN)).astype(I32), axis=0)
    rank = jnp.where(present, rank, -1)
    is_member = jnp.arange(MAXS, dtype=I32)[:, None] == rank[None, :]
    of_member = lambda v, zero: jnp.sum(
        jnp.where(is_member, jnp.sum(jnp.where(hit, v, zero), axis=1)[None, :], zero), axis=1
    )
    member_len, member_off, member_weight = of_member(all_len, 0), of_member(off, 0), of_member(all_weight, 0.0)

    ys = jnp.arange(NY, dtype=I32)[:, None, None]
    on_row = (((off + all_len)[None] + 3 - ys) >> 2) - ((off[None] + 3 - ys) >> 2)
    on_row = on_row.reshape(NY, NZ, NX * NC * SLOTS)
    goes = (all_dest.reshape(NZ, -1)[:, :, None] == gens[None, None, :]).astype(BF)
    load = jnp.einsum("yza,zad->yzd", on_row.astype(BF), goes, preferred_element_type=F32)
    most_along = jnp.max(jnp.sum(load.reshape(NY, NZ, NZ, NX * NC), axis=3))
    most_owned = jnp.max(jnp.sum(load, axis=1))
    fits = jnp.max(off[:, -1] + all_len[:, -1]) <= NY * CT
    choice = sum(jnp.where(fits & (most_along <= a) & (most_owned <= b), 0, 1) for a, b in ROOM)

    lo = (off + 3 - y) >> 2
    hi = (off + all_len + 3 - y) >> 2
    flat = lambda v: v.reshape(NZ, NX * NC * SLOTS)
    n, dz, do = flat(hi - lo), flat(all_dest) // (NX * NC), flat(all_dest) % (NX * NC)
    here = lambda v: lax.dynamic_index_in_dim(v, z, 0, keepdims=False)
    n0, d0 = here(n), here(dz)
    base = jnp.sum(jnp.where(before(n0.shape[0]) & (d0[:, None] == d0[None, :]), n0[:, None], 0), axis=0)
    add = (d0 * FAR + base - here(flat(lo))).reshape(NX * NC, SLOTS, 1)
    j = jnp.arange(CT, dtype=I32)[None, None, :]
    lo0, hi0 = (here(v.reshape(NZ, NX * NC, SLOTS))[:, :, None] for v in (lo, hi))
    at1 = jnp.sum(jnp.where((j >= lo0) & (j < hi0), add + j + 1, 0), axis=1) - 1
    n1 = jnp.where(dz == z, n, 0)
    base1 = prefix(n1)
    o = jnp.arange(NX * NC, dtype=I32)[None, :, None]
    by_owner = jnp.where(do[:, None, :] == o, n1[:, None, :], 0)
    earlier = jnp.sum(jnp.where(before(NZ)[:, :, None], jnp.sum(by_owner, axis=2)[:, None, :], 0), axis=0)
    base2 = prefix(by_owner) + earlier[:, :, None]
    base2 = jnp.sum(jnp.where(do[:, None, :] == o, base2, 0), axis=1)
    add = (do * FAR + base2 - base1)[:, :, None]
    k = jnp.arange(KT, dtype=I32)[None, None, :]
    inside = (k >= base1[:, :, None]) & (k < (base1 + n1)[:, :, None])
    at2 = jnp.sum(jnp.where(inside, add + k + 1, 0), axis=1) - 1
    yy = ys[:, :, 0]
    nm = ((member_off + member_len)[None] + 3 - yy) // 4 - (member_off[None] + 3 - yy) // 4
    basem = prefix(nm)[:, :, None]
    k = jnp.arange(KO, dtype=I32)[None, None, :]
    m = jnp.arange(MAXS, dtype=I32)[None, :, None]
    inside = (k >= basem) & (k < basem + nm[:, :, None])
    at3 = jnp.sum(jnp.where(inside, (k - basem) * MAXS + m + 1, 0), axis=1) - 1
    ok = (jnp.arange(POS, dtype=I32)[None, :, None] < nm[:, None, :]).reshape(SEQ, MAXS)

    def compacted(kt, ko):
        along = lax.all_to_all(sum_pack(summands, at1, kt), "z", split_axis=0, concat_axis=0, tiled=True)
        parts = repack(along, at2[:, :kt], ko).reshape(NX * NC * NY, ko, 128)
        tokens = lax.all_to_all(parts, ("x", "c", "y"), split_axis=0, concat_axis=0, tiled=True)
        return utility(tokens, ok, member_len, member_weight, at3[:, :ko])

    def as_they_are():
        dest = jnp.sum(jnp.where(slot_prompt[:, None] == gens[None, :], owner[None, :], 0), axis=1)
        return uncompacted(x, y, rows, chunks, dest, all_dest, (rank, member_len, member_weight))

    return lax.switch(choice, [functools.partial(compacted, *r) for r in ROOM] + [as_they_are])


def solution(mesh):
    fine = Mesh(mesh.devices.reshape(NZ, NX, NC, NY), ("z", "x", "c", "y"))
    g = ("z", "x", "c")
    placed = (P(None, g, "y"), P("y", g), P(g), P(g), P(g), P())
    return jax.shard_map(body, mesh=fine, in_specs=placed, out_specs=P(g, None), check_vma=False)
```

```python
import functools
import math

import jax
import jax.numpy as jnp
from jax import lax
from jax.experimental import pallas as pl
from jax.experimental.pallas import tpu as pltpu
from jax.sharding import Mesh
from jax.sharding import PartitionSpec as P

MAXS = 64
SEQ = 32
EMB = 1024
NZ, NX, NC, NY = 16, 4, 2, 4
GEN = NZ * NX * NC
SLOTS = 32
HB = 2048
BF = jnp.bfloat16
F32 = jnp.float32
I32 = jnp.int32
POS = SEQ // NY
CT = 192
ROOM = ((160, 320), (208, 352))
KT, KO = ROOM[-1]
FAR = 1024


def shift(v, axis, n, k):
    return lax.ppermute(v, axis, [(i, (i + k) % n) for i in range(n)])


def swap(v, axis, n, d):
    return lax.ppermute(v, axis, [(i, i ^ d) for i in range(n)])


def two_way_ring(v, axis, n):
    half = v.shape[0] // 2
    before = shift(v, axis, n, 1)
    after = shift(v, axis, n, n - 1)
    low = shift(before[:half], axis, n, 1)
    high = shift(after[half:], axis, n, n - 1)
    return [v, before, after, low, high]


RING = (0, NY - 1, 1, 2)


def best_match(rows, cols_ref, col_ref, unroll=1):

    def some(q, best):
        cols = cols_ref[pl.ds(pl.multiple_of(q * 512, 512), 512), :]
        s = lax.dot_general(rows, cols, (((1,), (1,)), ((), ())), preferred_element_type=F32)
        ok = col_ref[q] > 0
        for k in range(4):
            best = jnp.maximum(best, jnp.where(ok[k : k + 1], s[:, k * 128 : (k + 1) * 128], -2.0))
        return best

    best = lax.fori_loop(0, 4, some, jnp.full((rows.shape[0], 128), -2.0, F32), unroll=unroll)
    return jnp.maximum(best[:, :MAXS], best[:, MAXS:])


def finish(acc_ref, live_ref, len_ref, w_ref, out_ref):
    recall = acc_ref[...] / jnp.maximum(len_ref[...], 1.0)
    score = 0.5 * (recall + recall.T)
    util = jnp.sum(score * w_ref[...], axis=0, keepdims=True) / jnp.sum(w_ref[...])
    out_ref[...] = jnp.where(live_ref[...] > 0, util, 0.0)


def unit(v):
    s = lax.rsqrt(jnp.sum(v * v, axis=1, keepdims=True) * (1.0 / EMB) + 1e-6) * (1.0 / math.sqrt(EMB))
    return (v * s).astype(BF)


def utility_kernel(x_ref, row_ref, col_ref, live_ref, len_ref, w_ref, out_ref, xn_ref, acc_ref):
    i = pl.program_id(0)
    blk = row_ref.shape[0]

    @pl.when(i == 0)
    def _():
        acc_ref[...] = jnp.zeros_like(acc_ref)

        def norm(b, carry):
            at = pl.ds(pl.multiple_of(b * blk, blk), blk)
            xn_ref[at, :] = unit(x_ref[at, :].astype(F32))
            return carry

        lax.fori_loop(0, SEQ * MAXS // blk, norm, 0)

    best = best_match(xn_ref[pl.ds(pl.multiple_of(i * blk, blk), blk), :], xn_ref, col_ref)
    best = jnp.where(row_ref[...] > 0, best, 0.0)
    acc_ref[...] += jnp.sum(best.reshape(blk // MAXS, MAXS, MAXS), axis=0)

    @pl.when(i == pl.num_programs(0) - 1)
    def _():
        finish(acc_ref, live_ref, len_ref, w_ref, out_ref)


def packed_utility_kernel(x_ref, at_ref, col_ref, live_ref, len_ref, w_ref, out_ref, rows_ref, cols_ref, acc_ref):
    i = pl.program_id(0)
    room = at_ref.shape[2]

    @pl.when(i == 0)
    def _():
        acc_ref[...] = jnp.zeros_like(acc_ref)

        def place(q, carry):
            v = jnp.concatenate([x_ref[g * NY + q] for g in range(NX * NC)], axis=1)
            v = unit(v.astype(F32))
            rows_ref[q] = v
            slot = lax.broadcasted_iota(I32, (POS * MAXS, room), 0)
            pick = jnp.where(slot == at_ref[q], 1.0, 0.0).astype(BF)
            v = jnp.dot(pick, v, preferred_element_type=F32)
            cols_ref[pl.ds(pl.multiple_of(q * POS * MAXS, 512), POS * MAXS), :] = v.astype(BF)
            return carry

        lax.fori_loop(0, NY, place, 0)

    best = best_match(rows_ref[i], cols_ref, col_ref, unroll=4)
    at = at_ref[i]
    mine = (lax.broadcasted_iota(I32, (MAXS, room), 0) == at % MAXS) & (at >= 0)
    acc_ref[...] += jnp.dot(
        jnp.where(mine, 1.0, 0.0), best, precision=lax.Precision.HIGHEST, preferred_element_type=F32
    )

    @pl.when(i == pl.num_programs(0) - 1)
    def _():
        finish(acc_ref, live_ref, len_ref, w_ref, out_ref)


def utility(x, ok, member_len, member_weight, at=None):
    n = SEQ * MAXS
    whole = lambda a: pl.BlockSpec(a.shape, lambda i, d=a.ndim: (0,) * d)
    live = (member_len > 0).astype(F32)[None, :]
    small = [ok.astype(F32).reshape(4, n // 512, 128), live, member_len.astype(F32)[:, None], member_weight[:, None]]
    scratch = [pltpu.VMEM((n, EMB), BF), pltpu.VMEM((MAXS, MAXS), F32)]
    if at is None:
        kernel, steps = utility_kernel, 8
        side, spec = ok.astype(F32).reshape(n, 1), pl.BlockSpec((n // steps, 1), lambda i: (i, 0))
    else:
        kernel, steps = packed_utility_kernel, NY
        side = at[:, None, :]
        spec = whole(side)
        scratch = [pltpu.VMEM((NY, at.shape[1], EMB), BF)] + scratch
    return pl.pallas_call(
        kernel,
        grid=(steps,),
        in_specs=[whole(x), spec] + [whole(a) for a in small],
        out_specs=pl.BlockSpec((1, MAXS), lambda i: (0, 0)),
        out_shape=jax.ShapeDtypeStruct((1, MAXS), F32),
        scratch_shapes=scratch,
        compiler_params=pltpu.CompilerParams(vmem_limit_bytes=48 << 20),
    )(x, side, *small)


def with_meta_kernel(w_ref, prompt_ref, len_ref, weight_ref, out_ref):
    out_ref[:, :HB] = w_ref[...]
    row = lax.broadcasted_iota(I32, (8, SLOTS), 0)
    v = jnp.where(row == 0, prompt_ref[...].astype(F32), jnp.where(row == 1, len_ref[...].astype(F32), 0.0))
    v = jnp.where(row == 2, weight_ref[...].astype(F32), v)
    out_ref[:, HB:] = jnp.concatenate([v, jnp.zeros((8, 128 - SLOTS), F32)], axis=1).astype(BF)


def with_meta(w, prompt, length, weight):
    return pl.pallas_call(with_meta_kernel, out_shape=jax.ShapeDtypeStruct((8, HB + 128), BF))(
        w, prompt[None, :], length[None, :], weight[None, :]
    )


def project_kernel(pieces, where_ref, rows_ref, mate_ref, *refs):
    out_ref, meta_ref, both_ref = refs[-3:]
    c, first = where_ref[1], where_ref[2]
    refs = list(refs)
    for n, h in zip(pieces, (first, 1 - first)):
        o = 0
        for _ in range(n):
            w_ref = refs.pop(0)
            k = w_ref.shape[0]
            both_ref[pl.ds(pl.multiple_of(h * 128 + o, 64), k), :] = w_ref[:, :HB]
            meta_ref[h, 0, o : o + k, :] = w_ref[:, HB:]
            o += k
    for r_ref, e in ((rows_ref, c), (mate_ref, 1 - c)):
        term = lax.dot_general(r_ref[...], both_ref[...], (((1,), (1,)), ((), ())), preferred_element_type=F32)
        for h in range(2):
            for q in range(NY):
                out_ref[h, 0, q, e] = term[q * CT : (q + 1) * CT, h * 128 : (h + 1) * 128].astype(BF)


def project(at, c, rows, mate, ws, into):
    blocks = (2, 1, NY, NC, CT, 128), (2, 1, 128, 128)
    whole = lambda a: pl.BlockSpec(a.shape, lambda i, at: (0, 0))
    old = [] if into is None else list(into)
    flat = [w for pair in ws for w in pair]
    n = 3 + len(flat)
    return pl.pallas_call(
        functools.partial(project_kernel, [len(pair) for pair in ws]),
        grid_spec=pltpu.PrefetchScalarGridSpec(
            num_scalar_prefetch=1,
            grid=(1,),
            in_specs=[whole(a) for a in (rows, mate, *flat)] + [pl.BlockSpec(memory_space=pl.ANY) for _ in old],
            out_specs=[pl.BlockSpec(b, lambda i, at, d=len(b): (0, at[0]) + (0,) * (d - 2)) for b in blocks],
            scratch_shapes=[pltpu.VMEM((256, HB), BF)],
        ),
        out_shape=[jax.ShapeDtypeStruct((2, 2) + b[2:], BF) for b in blocks],
        input_output_aliases={n: 0, n + 1: 1} if old else {},
        compiler_params=pltpu.CompilerParams(vmem_limit_bytes=40 << 20),
        cost_estimate=pl.CostEstimate(flops=2 * NC * NY * CT * HB * 256, transcendentals=0, bytes_accessed=8 << 20),
    )(jnp.stack([at % 2, c, at // 2]).astype(I32), rows, mate, *flat, *old)


def sum_pack_kernel(x_ref, at_ref, out_ref, v_ref):
    i = pl.program_id(0)
    some, room = out_ref.shape[:2]

    @pl.when(i == 0)
    def _():

        def add(g, carry):
            for e in range(NC):
                v = x_ref[g * NY, e].astype(F32)
                for q in range(1, NY):
                    v = v + x_ref[g * NY + q, e].astype(F32)
                v_ref[pl.ds(pl.multiple_of((g * NC + e) * CT, 64), CT), :] = v.astype(BF)
            return carry

        lax.fori_loop(0, NX, add, 0)

    def bucket(b, carry):
        slot = lax.broadcasted_iota(I32, (room, NX * NC * CT), 0) + (i * some + b) * FAR
        pick = jnp.where(slot == at_ref[...], 1.0, 0.0).astype(BF)
        out_ref[b] = jnp.dot(pick, v_ref[...], preferred_element_type=F32).astype(BF)
        return carry

    lax.fori_loop(0, some, bucket, 0)


def sum_pack(x, at, room):
    n = NX * NC * CT
    some = 4
    return pl.pallas_call(
        sum_pack_kernel,
        grid=(NZ // some,),
        in_specs=[pl.BlockSpec(x.shape, lambda i: (0, 0, 0, 0)), pl.BlockSpec((1, n), lambda i: (0, 0))],
        out_specs=pl.BlockSpec((some, room, 128), lambda i: (i, 0, 0)),
        out_shape=jax.ShapeDtypeStruct((NZ, room, 128), BF),
        scratch_shapes=[pltpu.VMEM((n, 128), BF)],
        compiler_params=pltpu.CompilerParams(vmem_limit_bytes=40 << 20),
    )(x, at.reshape(1, n))


def repack_kernel(x_ref, at_ref, out_ref):
    i = pl.program_id(0)
    some, _, room = out_ref.shape[:3]

    def owner(b, carry):
        slot = lax.broadcasted_iota(I32, (room, x_ref.shape[0]), 0) + (i * some + b) * FAR
        pick = jnp.where(slot == at_ref[...], 1.0, 0.0).astype(BF)
        v = jnp.dot(pick, x_ref[...], preferred_element_type=F32).astype(BF)
        for q in range(NY):
            out_ref[b, q] = v
        return carry

    lax.fori_loop(0, some, owner, 0)


def repack(x, at, room):
    n = x.shape[0] * x.shape[1]
    some = 2
    return pl.pallas_call(
        repack_kernel,
        grid=(NX * NC // some,),
        in_specs=[pl.BlockSpec((n, 128), lambda i: (0, 0)), pl.BlockSpec((1, n), lambda i: (0, 0))],
        out_specs=pl.BlockSpec((some, NY, room, 128), lambda i: (i, 0, 0, 0)),
        out_shape=jax.ShapeDtypeStruct((NX * NC, NY, room, 128), BF),
        compiler_params=pltpu.CompilerParams(vmem_limit_bytes=40 << 20),
    )(x.reshape(n, 128), at.reshape(1, n))


def before(n):
    i = jnp.arange(n, dtype=I32)
    return i[:, None] < i[None, :]


def prefix(v):
    return jnp.dot(v.astype(BF), before(v.shape[-1]).astype(BF), preferred_element_type=F32).astype(I32)


def uncompacted(x, y, rows, chunks, dest, all_dest, member):
    rank, member_len, member_weight = member
    projected = jnp.zeros((NX, SEQ * SLOTS, NC * 128), BF)
    c = lax.axis_index("c")
    for k, chunk in zip(RING, chunks[:3] + [jnp.concatenate(chunks[3:])]):
        other = swap(chunk, "c", NC, 1)
        both = jnp.concatenate([jnp.where(c == 1, other, chunk), jnp.where(c == 1, chunk, other)])
        term = lax.dot_general(rows, both[:, :HB], (((1,), (1,)), ((), ())), preferred_element_type=F32)
        projected = lax.dynamic_update_slice(projected, term.astype(BF)[None], ((x + k) % NX, 0, 0))

    by_pos = projected.reshape(NX, NY, POS * SLOTS, NC * 128)
    total = lax.dynamic_index_in_dim(by_pos, y, 1, keepdims=False).astype(F32)
    for k in (1, 3, 2):
        piece = lax.dynamic_index_in_dim(by_pos, (y + k) % NY, 1, keepdims=False)
        total = total + shift(piece, "y", NY, k).astype(F32)
    emb = total.astype(BF).transpose(1, 0, 2).reshape(POS * SLOTS, EMB)

    out_row = jnp.arange(GEN * POS, dtype=I32)
    in_row = jnp.arange(POS, dtype=I32)[:, None] + dest[None, :] * POS
    pick = (out_row[:, None] == in_row.reshape(1, -1)).astype(BF)
    send = jnp.dot(pick, emb, preferred_element_type=F32).astype(BF).reshape(GEN, POS, EMB)
    arrived = lax.all_to_all(send, ("z", "x", "c"), split_axis=0, concat_axis=0, tiled=True)
    src_at = jnp.where(rank[:, None] >= 0, jnp.arange(POS, dtype=I32)[None, :] * MAXS + rank[:, None], -1)
    pick = (jnp.arange(POS * MAXS, dtype=I32)[:, None] == src_at.reshape(1, -1)).astype(BF)
    mine = jnp.dot(pick, arrived.reshape(GEN * POS, EMB), preferred_element_type=F32).astype(BF)

    tokens = jnp.concatenate(two_way_ring(mine, "y", NY))
    pos = jnp.concatenate([((y + k) % NY) * POS + jnp.arange(POS, dtype=I32) for k in RING])
    return utility(tokens, pos[:, None] < member_len[None, :], member_len, member_weight)


def body(hidden, w_proj, slot_prompt, lengths, weights, owner):
    z, x, c, y = (lax.axis_index(a) for a in ("z", "x", "c", "y"))
    me = (z * NX + x) * NC + c
    gens = jnp.arange(GEN, dtype=I32)

    part = with_meta(w_proj.T, slot_prompt, lengths, weights)
    part = lax.all_gather(part, "z", axis=0, tiled=True)
    lens, part = lax.optimization_barrier((lengths, part))

    rows = hidden.reshape(SEQ * SLOTS, HB)
    start = jnp.sum(jnp.where(before(SLOTS), lens[:, None], 0), axis=0)
    t = jnp.arange(SEQ, dtype=I32)[:, None]
    at = t + start[None, :]
    at = jnp.where((t < lens[None, :]) & (at < NY * CT), (at % NY) * CT + at // NY, -1)
    pick = (jnp.arange(NY * CT, dtype=I32)[:, None] == at.reshape(1, -1)).astype(BF)
    chunks = two_way_ring(part, "x", NX)
    packed = jnp.dot(pick, rows, preferred_element_type=F32).astype(BF)
    own, prev, after, low, high = chunks
    packed, prev, after = lax.optimization_barrier((packed, prev, after))
    mate = swap(packed, "c", NC, 1)
    made = project((x + NX - 1) % NX, c, packed, mate, ((prev,), (after,)), None)
    send, metas = project(x, c, packed, mate, ((own,), (low, high)), made)
    summands = lax.all_to_all(
        send.reshape(NX * NY, NC, CT, 128), ("x", "y"), split_axis=0, concat_axis=0, tiled=True
    )

    metas = metas.reshape(NX, NZ, 8, 128)[:, :, :3]
    twin = swap(metas, "c", NC, 1)
    metas = jnp.stack([jnp.where(c == 1, twin, metas), jnp.where(c == 1, metas, twin)], axis=2)
    metas = metas.transpose(3, 1, 0, 2, 4).reshape(3, GEN, 128)[:, :, :SLOTS]
    all_prompt = metas[0].astype(I32)
    all_len = metas[1].astype(I32)
    all_weight = metas[2].astype(F32)
    all_dest = jnp.sum(jnp.where(all_prompt[:, :, None] == gens, owner, 0), axis=2)
    off = prefix(all_len)

    hit = all_dest == me
    present = jnp.any(hit, axis=1)
    rank = jnp.sum((present[:, None] & before(GEN)).astype(I32), axis=0)
    rank = jnp.where(present, rank, -1)
    is_member = jnp.arange(MAXS, dtype=I32)[:, None] == rank[None, :]
    of_member = lambda v, zero: jnp.sum(
        jnp.where(is_member, jnp.sum(jnp.where(hit, v, zero), axis=1)[None, :], zero), axis=1
    )
    member_len, member_off, member_weight = of_member(all_len, 0), of_member(off, 0), of_member(all_weight, 0.0)

    ys = jnp.arange(NY, dtype=I32)[:, None, None]
    on_row = (((off + all_len)[None] + 3 - ys) >> 2) - ((off[None] + 3 - ys) >> 2)
    on_row = on_row.reshape(NY, NZ, NX * NC * SLOTS)
    goes = (all_dest.reshape(NZ, -1)[:, :, None] == gens[None, None, :]).astype(BF)
    load = jnp.einsum("yza,zad->yzd", on_row.astype(BF), goes, preferred_element_type=F32)
    most_along = jnp.max(jnp.sum(load.reshape(NY, NZ, NZ, NX * NC), axis=3))
    most_owned = jnp.max(jnp.sum(load, axis=1))
    fits = jnp.max(off[:, -1] + all_len[:, -1]) <= NY * CT
    choice = sum(jnp.where(fits & (most_along <= a) & (most_owned <= b), 0, 1) for a, b in ROOM)

    lo = (off + 3 - y) >> 2
    hi = (off + all_len + 3 - y) >> 2
    flat = lambda v: v.reshape(NZ, NX * NC * SLOTS)
    n, dz, do = flat(hi - lo), flat(all_dest) // (NX * NC), flat(all_dest) % (NX * NC)
    here = lambda v: lax.dynamic_index_in_dim(v, z, 0, keepdims=False)
    n0, d0 = here(n), here(dz)
    base = jnp.sum(jnp.where(before(n0.shape[0]) & (d0[:, None] == d0[None, :]), n0[:, None], 0), axis=0)
    add = (d0 * FAR + base - here(flat(lo))).reshape(NX * NC, SLOTS, 1)
    j = jnp.arange(CT, dtype=I32)[None, None, :]
    lo0, hi0 = (here(v.reshape(NZ, NX * NC, SLOTS))[:, :, None] for v in (lo, hi))
    at1 = jnp.sum(jnp.where((j >= lo0) & (j < hi0), add + j + 1, 0), axis=1) - 1
    n1 = jnp.where(dz == z, n, 0)
    base1 = prefix(n1)
    o = jnp.arange(NX * NC, dtype=I32)[None, :, None]
    by_owner = jnp.where(do[:, None, :] == o, n1[:, None, :], 0)
    earlier = jnp.sum(jnp.where(before(NZ)[:, :, None], jnp.sum(by_owner, axis=2)[:, None, :], 0), axis=0)
    base2 = prefix(by_owner) + earlier[:, :, None]
    base2 = jnp.sum(jnp.where(do[:, None, :] == o, base2, 0), axis=1)
    add = (do * FAR + base2 - base1)[:, :, None]
    k = jnp.arange(KT, dtype=I32)[None, None, :]
    inside = (k >= base1[:, :, None]) & (k < (base1 + n1)[:, :, None])
    at2 = jnp.sum(jnp.where(inside, add + k + 1, 0), axis=1) - 1
    yy = ys[:, :, 0]
    nm = ((member_off + member_len)[None] + 3 - yy) // 4 - (member_off[None] + 3 - yy) // 4
    basem = prefix(nm)[:, :, None]
    k = jnp.arange(KO, dtype=I32)[None, None, :]
    m = jnp.arange(MAXS, dtype=I32)[None, :, None]
    inside = (k >= basem) & (k < basem + nm[:, :, None])
    at3 = jnp.sum(jnp.where(inside, (k - basem) * MAXS + m + 1, 0), axis=1) - 1
    ok = (jnp.arange(POS, dtype=I32)[None, :, None] < nm[:, None, :]).reshape(SEQ, MAXS)

    def compacted(kt, ko):
        along = lax.all_to_all(sum_pack(summands, at1, kt), "z", split_axis=0, concat_axis=0, tiled=True)
        parts = repack(along, at2[:, :kt], ko).reshape(NX * NC * NY, ko, 128)
        tokens = lax.all_to_all(parts, ("x", "c", "y"), split_axis=0, concat_axis=0, tiled=True)
        return utility(tokens, ok, member_len, member_weight, at3[:, :ko])

    def as_they_are():
        dest = jnp.sum(jnp.where(slot_prompt[:, None] == gens[None, :], owner[None, :], 0), axis=1)
        return uncompacted(x, y, rows, chunks, dest, all_dest, (rank, member_len, member_weight))

    return lax.switch(choice, [functools.partial(compacted, *r) for r in ROOM] + [as_they_are])


def solution(mesh):
    fine = Mesh(mesh.devices.reshape(NZ, NX, NC, NY), ("z", "x", "c", "y"))
    g = ("z", "x", "c")
    placed = (P(None, g, "y"), P("y", g), P(g), P(g), P(g), P())
    return jax.shard_map(body, mesh=fine, in_specs=placed, out_specs=P(g, None), check_vma=False)
```
